256 devices in a mesh: dp: 16 (over x, y), shard: 16 (over z, core).
Axes of the slice: x: 4, y: 4, z: 8, core: 2. Of those that a mesh axis runs over, the one named last changes fastest.
Arguments:
- gradient: bfloat16 [16, 4096, 6144], P('dp', None, 'shard'), may hold values from -400 to 400
- error_buffer: bfloat16 [16, 4096, 6144], P('dp', None, 'shard'), may hold values from -6 to 6
- right_init: float32 [6144, 32], P('shard'), may hold values from -6 to 6
- first_moment: float32 [4096, 6144], P(('dp', 'shard')), may hold values from -0.06 to 0.06
- second_moment: float32 [4096, 6144], P(('dp', 'shard')), may hold values from 0.001 to 0.01
Outputs:
- error_out: bfloat16 [16, 4096, 6144], P('dp', None, 'shard')
- first_out: float32 [4096, 6144], P(('dp', 'shard'))
- second_out: float32 [4096, 6144], P(('dp', 'shard'))
- direction: float32 [4096, 6144], P(('dp', 'shard'))
The draws below stay inside these ranges and needn't reach their ends.
All inputs are finite; a program needn't handle non-finite values.
Results may differ from the reference program's by a relative error of at most 0.009.
Values sent between devices are 32-bit elements; how exact they have to be, the bound alone decides.
A program may use at most 64 MiB of HBM per device.

```python
import math
import jax
import jax.numpy as jnp
from jax import lax

D = 4096
F = 6144
R = 32
REPLICAS = 16


def draw_gradient(key, part):
    base = jax.random.fold_in(key, 11)
    key_rows, key_cols, key_sample = jax.random.split(base, 3)
    rising = 6.0 ** (jnp.arange(D, dtype=jnp.float32) / D)
    row_scale = rising * jnp.exp(jax.random.uniform(key_rows, (D,), jnp.float32, 0.0, math.log(10.0) / 4))
    col_scale = jnp.exp(jax.random.uniform(key_cols, (F,), jnp.float32, 0.0, math.log(10.0) / 2))
    sample = jnp.clip(jax.random.normal(key_sample, (REPLICAS, D, F), jnp.float32), -6.0, 6.0)
    factor = jnp.sqrt(jnp.float32(REPLICAS) / 16.0)
    sample = factor * sample
    return (sample * row_scale[None, :, None] * col_scale[None, None, :]).astype(jnp.bfloat16)


def draw_error_buffer(key, part):
    base = jax.random.fold_in(key, 23)
    key_sample = jax.random.fold_in(base, 0)
    factor = jnp.sqrt(jnp.float32(REPLICAS) / 16.0)
    sample = jnp.clip(jax.random.normal(key_sample, (REPLICAS, D, F), jnp.float32), -6.0, 6.0)
    values = factor * sample
    return values.astype(jnp.bfloat16)


def levels(rng, extent, pieces, low, high):
    factor_of = 1.0
    for position, shards_of in pieces:
        heights = jax.random.uniform(jax.random.fold_in(jax.random.fold_in(rng, 6), position), (shards_of,), jnp.float32, low / len(pieces), high / len(pieces))
        factor_of = factor_of * jnp.repeat(jnp.exp(heights), extent[position] // shards_of).reshape((-1,) + (1,) * (len(extent) - 1 - position))
    return factor_of


def normal_values(key, extent, spread, most, cuts=(), held_as=jnp.bfloat16):
    array = jax.random.normal(key, extent, jnp.float32) * spread
    if len(cuts) > 0:
        array = levels(key, extent, cuts, -0.22, 0.18) * array
    return jnp.clip(array, min=-most, max=most).astype(held_as)


def setup_inputs(seed: int = 0) -> dict:
    seeds = jax.random.split(jax.random.key(seed), 6)
    return {
        "gradient": draw_gradient(jax.random.fold_in(seeds[5], 71), 0),
        "error_buffer": draw_error_buffer(jax.random.fold_in(seeds[5], 71), 0),
        "right_init": normal_values(seeds[2], (F, R), 1.0, 6.0, ((0, 16),), jnp.float32),
        "first_moment": normal_values(seeds[3], (D, F), 0.01, 0.06, ((0, 256),), jnp.float32),
        "second_moment": jnp.clip(jnp.exp(math.log(0.01) - 2.30258502 * jax.random.uniform(seeds[4], (D, F), jnp.float32) ** levels(seeds[4], (D, F), ((0, 256),), -0.2, 0.2)), 0.001, 0.01),
    }


CLIP_LEVEL = 0.9
BETA_ONE = 0.9
BETA_TWO = 0.95
EPSILON = 1e-08

def orthonormal(left_raw, gram_matrix):
    width = gram_matrix.shape[0]
    ridge_shift = 1e-06 * jnp.trace(gram_matrix) / width
    lower_factor = jnp.linalg.cholesky(gram_matrix + ridge_shift * jnp.eye(width, dtype=jnp.float32))
    return lax.linalg.triangular_solve(lower_factor, left_raw, left_side=False, lower=True, transpose_a=True)

def merge_pair(items):
    return (items[0].astype(jnp.float32) + items[1].astype(jnp.float32)).astype(jnp.bfloat16)

def reference(gradient, error_buffer, right_init, first_moment, second_moment):
    merged = lax.map(merge_pair, (gradient, error_buffer))
    right_low = right_init.astype(jnp.bfloat16)

    def left_term(matrix):
        return jnp.dot(matrix.astype(jnp.float32), right_low.astype(jnp.float32), preferred_element_type=jnp.float32)
    left_raw = lax.optimization_barrier(jnp.sum(lax.map(left_term, merged), axis=0)) / REPLICAS
    gram_matrix = jnp.dot(left_raw.T, left_raw, precision=lax.Precision.HIGHEST)
    left_orth = orthonormal(left_raw, gram_matrix)
    left_low = left_orth.astype(jnp.bfloat16)

    def right_term(matrix):
        return lax.dot_general(matrix.astype(jnp.float32), left_low.astype(jnp.float32), (((0,), (0,)), ((), ())), preferred_element_type=jnp.float32)
    right_new = lax.optimization_barrier(jnp.sum(lax.map(right_term, merged), axis=0)) / REPLICAS
    update = jnp.dot(left_orth, right_new.T, precision=lax.Precision.HIGHEST)

    def residual(matrix):
        return (matrix.astype(jnp.float32) - update).astype(jnp.bfloat16)
    error_out = lax.map(residual, merged)
    grad_norm = jnp.sqrt(jnp.sum(update * update))
    clip_level = CLIP_LEVEL * jnp.sqrt(jnp.float32(R * (D + F)))
    scaled = update * (clip_level / jnp.maximum(grad_norm, clip_level))
    first_out = BETA_ONE * first_moment + (1.0 - BETA_ONE) * scaled
    second_out = BETA_TWO * second_moment + (1.0 - BETA_TWO) * scaled * scaled
    direction = first_out / (jnp.sqrt(second_out) + EPSILON)
    return (error_out, first_out, second_out, direction)
```

```python
import jax
import jax.numpy as jnp
from jax import lax
from jax.experimental import pallas as pl
from jax.experimental.pallas import tpu as pltpu
from jax.sharding import PartitionSpec as P

D = 4096
F = 6144
R = 32
DP = 16
SH = 16
ZN = 8
CHUNKS = 8
ROWS = D // CHUNKS
COLS = F // SH
OWN = D // (DP * SH)

CLIP_LEVEL = 0.9
BETA_ONE = 0.9
BETA_TWO = 0.95
EPSILON = 1e-08

MESH = pl.DeviceIdType.MESH
F32 = jnp.float32
BF16 = jnp.bfloat16
NT = (((1,), (1,)), ((), ()))
NN = (((1,), (0,)), ((), ()))


def mm(a, b, dims):
    return lax.dot_general(a, b, dims, preferred_element_type=F32)


def split(x):
    high = x.astype(BF16)
    rest = x - high.astype(F32)
    mid = rest.astype(BF16)
    low = (rest - mid.astype(F32)).astype(BF16)
    return high, mid, low


def gram(parts):
    stack = jnp.concatenate(parts, axis=0)
    full = mm(stack, stack, NT)
    n = len(parts)
    rows = sum(full[R * a : R * (a + 1)] for a in range(n))
    return sum(rows[:, R * a : R * (a + 1)] for a in range(n))


def triangular_inverse(gram_matrix):
    row = lax.broadcasted_iota(jnp.int32, (R, R), 0)
    col = lax.broadcasted_iota(jnp.int32, (R, R), 1)
    eye = row == col
    trace = jnp.sum(jnp.where(eye, gram_matrix, 0.0), keepdims=True)
    shifted = gram_matrix + jnp.where(eye, 1e-06 * trace / R, 0.0)
    work = jnp.concatenate([shifted, jnp.where(eye, 1.0, 0.0)], axis=1)
    wide_row = lax.broadcasted_iota(jnp.int32, (R, 2 * R), 0)
    wide_col = lax.broadcasted_iota(jnp.int32, (R, 2 * R), 1)
    for k in range(R - 1):
        column = jnp.broadcast_to(work[:, k : k + 1], (R, 2 * R))
        pivot = column[k : k + 1]
        line = work[k : k + 1] * (1.0 / pivot)
        work = work - jnp.where(wide_row > k, column, 0.0) * line
    diagonal = jnp.sum(jnp.where(wide_row == wide_col, work, 0.0), axis=1, keepdims=True)
    return work[:, R : 2 * R] * lax.rsqrt(diagonal)


def kernel(
    right_ref, grad_hbm, errb_hbm, first_hbm, second_hbm,
    err_hbm, first_out_hbm, second_out_hbm, direction_hbm,
    grad_buf, errb_buf, merged, part, core_in, half, dp_in, z_out, z_in, z_all, left_raw,
    left_split, left_stack, right_out, right_in, right_all, blocks, owned,
    first_buf, second_buf, first_res, second_res, direction_res,
    load_g, load_e, load_m,
    s_core, r_core, s_dp, r_dp, s_z, r_z, s_za, r_za, s_dpa, r_dpa, s_ca, r_ca,
    s_rr, r_rr, s_ra, r_ra, s_bz, r_bz, s_bc, r_bc, out_e, out_m,
):
    i = lax.axis_index("dp")
    j = lax.axis_index("shard")
    x, y = i // 4, i % 4
    z, c = j // 2, j % 2
    other = j + 1 - 2 * c

    def dp_peer(d):
        return ((x + d // 4) % 4) * 4 + (y + d % 4) % 4

    def z_peer(d):
        return (z + d) % ZN

    def remote(src, dst, ss, rs, dp, sh):
        return pltpu.make_async_remote_copy(
            src_ref=src, dst_ref=dst, send_sem=ss, recv_sem=rs, device_id=(dp, sh), device_id_type=MESH
        )

    barrier = pltpu.get_barrier_semaphore()

    loads = []
    for k in range(CHUNKS):
        chunk = (k + (CHUNKS // 2) * (1 - c)) % CHUNKS
        a = pltpu.make_async_copy(grad_hbm.at[chunk], grad_buf.at[chunk], load_g.at[k])
        b = pltpu.make_async_copy(errb_hbm.at[chunk], errb_buf.at[chunk], load_e.at[k])
        a.start()
        b.start()
        loads.append((chunk, a, b))
    for d in range(1, DP):
        pl.semaphore_signal(barrier, inc=1, device_id=(dp_peer(d), j), device_id_type=MESH)
    for d in range(1, ZN):
        pl.semaphore_signal(barrier, inc=1, device_id=(i, 2 * z_peer(d) + c), device_id_type=MESH)
    pl.semaphore_signal(barrier, inc=1, device_id=(i, other), device_id_type=MESH)
    load_first = pltpu.make_async_copy(first_hbm, first_buf, load_m.at[0])
    load_second = pltpu.make_async_copy(second_hbm, second_buf, load_m.at[1])

    right_low = right_ref[...].astype(BF16)
    sends = []
    for k in range(CHUNKS):
        chunk, a, b = loads[k]
        a.wait()
        b.wait()
        total = (grad_buf[chunk].astype(F32) + errb_buf[chunk].astype(F32)).astype(BF16)
        merged[chunk] = total
        product = mm(right_low, total, NT)
        for t in range(4):
            part[4 * chunk + t] = product[:, 128 * t : 128 * (t + 1)]
        if k == 0:
            pl.semaphore_wait(barrier, DP - 1 + ZN - 1 + 1)
        if k < CHUNKS // 2:
            copy = remote(
                part.at[pl.ds(4 * chunk, 4)], core_in.at[pl.ds(4 * k, 4)], s_core.at[k], r_core.at[k], i, other
            )
            copy.start()
            sends.append(copy)
        else:
            q = k - CHUNKS // 2
            remote(
                part.at[pl.ds(4 * chunk, 4)], core_in.at[pl.ds(4 * q, 4)], s_core.at[q], r_core.at[q], i, other
            ).wait_recv()
            for t in range(4):
                half[4 * q + t] = part[4 * chunk + t] + core_in[4 * q + t]
    load_first.start()
    load_second.start()

    for d in range(1, DP):
        p = dp_peer(d)
        copy = remote(half.at[p], dp_in.at[i], s_dp.at[d], r_dp.at[i], p, j)
        copy.start()
        sends.append(copy)
    dp_in[i] = half[i]
    for d in range(1, DP):
        p = dp_peer(d)
        remote(half.at[p], dp_in.at[p], s_dp.at[d], r_dp.at[p], p, j).wait_recv()
    total = dp_in[0]
    for p in range(1, DP):
        total = total + dp_in[p]
    for k in range(ZN):
        z_out[k] = total[4 * k : 4 * (k + 1)]
    for d in range(1, ZN):
        p = z_peer(d)
        copy = remote(z_out.at[p], z_in.at[z], s_z.at[d], r_z.at[z], i, 2 * p + c)
        copy.start()
        sends.append(copy)
    z_in[z] = z_out[z]
    for d in range(1, ZN):
        p = z_peer(d)
        remote(z_out.at[p], z_in.at[p], s_z.at[d], r_z.at[p], i, 2 * p + c).wait_recv()
    total = z_in[0]
    for p in range(1, ZN):
        total = total + z_in[p]
    z_all[z] = total * (1.0 / DP)

    for d in range(1, ZN):
        p = z_peer(d)
        copy = remote(z_all.at[z], z_all.at[z], s_za.at[d], r_za.at[z], i, 2 * p + c)
        copy.start()
        sends.append(copy)
    for d in range(1, ZN):
        p = z_peer(d)
        remote(z_all.at[p], z_all.at[p], s_za.at[d], r_za.at[p], i, 2 * p + c).wait_recv()
    mine = DP * c + i
    for k in range(ZN):
        left_raw[mine, pl.ds(4 * k, 4), :] = z_all[k]
    for d in range(1, DP):
        p = dp_peer(d)
        copy = remote(left_raw.at[mine], left_raw.at[mine], s_dpa.at[d], r_dpa.at[i], p, j)
        copy.start()
        sends.append(copy)
    copy = remote(left_raw.at[mine], left_raw.at[mine], s_ca.at[i], r_ca.at[i], i, other)
    copy.start()
    sends.append(copy)
    for d in range(1, DP):
        p = dp_peer(d)
        q = DP * c + p
        remote(left_raw.at[q], left_raw.at[q], s_dpa.at[d], r_dpa.at[p], p, j).wait_recv()
        copy = remote(left_raw.at[q], left_raw.at[q], s_ca.at[p], r_ca.at[p], i, other)
        copy.start()
        sends.append(copy)
    for p in range(DP):
        q = DP * (1 - c) + p
        remote(left_raw.at[q], left_raw.at[q], s_ca.at[p], r_ca.at[p], i, other).wait_recv()

    gram_matrix = jnp.zeros((R, R), F32)
    for k in range(CHUNKS):
        wide = jnp.concatenate([left_raw[4 * k + t] for t in range(4)], axis=1)
        parts = split(wide)
        for n in range(3):
            left_split[k, n] = parts[n]
        gram_matrix = gram_matrix + gram(parts)
    inverse = split(triangular_inverse(gram_matrix))
    inverse = jnp.concatenate([jnp.concatenate([t] * 3, axis=1) for t in inverse], axis=0)

    right_part = jnp.zeros((R, COLS), F32)
    for k in range(CHUNKS):
        stack = jnp.concatenate([left_split[k, n] for n in range(3)], axis=0)
        wide = mm(inverse, stack, NN)
        parts = split(wide[:R] + wide[R : 2 * R] + wide[2 * R :])
        for n in range(3):
            left_split[k, n] = parts[n]
        right_part = right_part + mm(parts[0], merged[k], NN)
    for p in range(DP):
        right_out[p] = right_part[2 * p : 2 * p + 2]
    for d in range(1, DP):
        p = dp_peer(d)
        copy = remote(right_out.at[p], right_in.at[i], s_rr.at[d], r_rr.at[i], p, j)
        copy.start()
        sends.append(copy)
    right_in[i] = right_out[i]
    ortho_gram = jnp.zeros((R, R), F32)
    for k in range(CHUNKS):
        high, mid, low = (left_split[k, n] for n in range(3))
        ortho_gram = ortho_gram + gram((high, mid, low))
        left_stack[k] = jnp.concatenate([high, high, mid, mid], axis=0).T
    for d in range(1, DP):
        p = dp_peer(d)
        remote(right_out.at[p], right_in.at[p], s_rr.at[d], r_rr.at[p], p, j).wait_recv()
    total = right_in[0]
    for p in range(1, DP):
        total = total + right_in[p]
    right_all[i] = total * (1.0 / DP)
    for d in range(1, DP):
        p = dp_peer(d)
        copy = remote(right_all.at[i], right_all.at[i], s_ra.at[d], r_ra.at[i], p, j)
        copy.start()
        sends.append(copy)
    for d in range(1, DP):
        p = dp_peer(d)
        remote(right_all.at[p], right_all.at[p], s_ra.at[d], r_ra.at[p], p, j).wait_recv()
    for p in range(DP):
        blocks[j, pl.ds(2 * p, 2), :] = right_all[p]

    for d in range(1, ZN):
        p = z_peer(d)
        copy = remote(blocks.at[j], blocks.at[j], s_bz.at[d], r_bz.at[z], i, 2 * p + c)
        copy.start()
        sends.append(copy)
    copy = remote(blocks.at[j], blocks.at[j], s_bc.at[z], r_bc.at[z], i, other)
    copy.start()
    sends.append(copy)

    high, mid, low = split(blocks[j])
    mine_stack = jnp.concatenate([high, mid, high, mid], axis=0)
    outs = []
    for k in range(CHUNKS):
        update = mm(left_stack[k], mine_stack, NN)
        errb_buf[k] = (merged[k].astype(F32) - update).astype(BF16)
        copy = pltpu.make_async_copy(errb_buf.at[k], err_hbm.at[k], out_e.at[k])
        copy.start()
        outs.append(copy)
        if k > 0:
            p = z_peer(k)
            q = 2 * p + c
            remote(blocks.at[q], blocks.at[q], s_bz.at[k], r_bz.at[p], i, q).wait_recv()
            copy = remote(blocks.at[q], blocks.at[q], s_bc.at[p], r_bc.at[p], i, other)
            copy.start()
            sends.append(copy)
    for p in range(ZN):
        q = 2 * p + 1 - c
        remote(blocks.at[q], blocks.at[q], s_bc.at[p], r_bc.at[p], i, other).wait_recv()

    tile = 2 * i + j // 8
    first_lane = OWN * (j % 8)
    pick = (
        lax.broadcasted_iota(jnp.int32, (OWN, 128), 1) == lax.broadcasted_iota(jnp.int32, (OWN, 128), 0) + first_lane
    )
    pick = jnp.where(pick, 1.0, 0.0).astype(BF16)
    lane_tile = tile % 4
    chunk = tile // 4
    own = []
    for n in range(2):
        whole = left_split[chunk, n]
        rows = mm(pick, whole[:, 0:128], NT) * jnp.where(lane_tile == 0, 1.0, 0.0)
        for t in range(1, 4):
            rows = rows + mm(pick, whole[:, 128 * t : 128 * (t + 1)], NT) * jnp.where(lane_tile == t, 1.0, 0.0)
        own.append(rows.astype(BF16))
    own_stack = jnp.concatenate([own[0], own[0], own[1], own[1]], axis=1)
    square = jnp.zeros((R, R), F32)
    for q in range(SH):
        high, mid, low = split(blocks[q])
        square = square + gram((high, mid))
        owned[:, COLS * q : COLS * (q + 1)] = mm(own_stack, jnp.concatenate([high, mid, high, mid], axis=0), NN)
    norm = jnp.sqrt(jnp.sum(square * ortho_gram, keepdims=True))
    clip_level = CLIP_LEVEL * (float(R * (D + F)) ** 0.5)
    scale = clip_level / jnp.maximum(norm, clip_level)
    load_first.wait()
    load_second.wait()
    for q in range(SH):
        lanes = slice(COLS * q, COLS * (q + 1))
        scaled = owned[:, lanes] * scale
        first = BETA_ONE * first_buf[:, lanes] + (1.0 - BETA_ONE) * scaled
        second = BETA_TWO * second_buf[:, lanes] + (1.0 - BETA_TWO) * scaled * scaled
        first_res[:, lanes] = first
        second_res[:, lanes] = second
        direction_res[:, lanes] = first / (jnp.sqrt(second) + EPSILON)
    for n, (res, hbm) in enumerate(
        ((first_res, first_out_hbm), (second_res, second_out_hbm), (direction_res, direction_hbm))
    ):
        copy = pltpu.make_async_copy(res, hbm, out_m.at[n])
        copy.start()
        outs.append(copy)
    for copy in sends:
        copy.wait_send()
    for copy in outs:
        copy.wait()


def local(gradient, error_buffer, right_init, first_moment, second_moment):
    shape3 = (CHUNKS, ROWS, COLS)
    dma = pltpu.SemaphoreType.DMA
    vmem = pltpu.VMEM
    err, first, second, direction = pl.pallas_call(
        kernel,
        out_shape=(
            jax.ShapeDtypeStruct(shape3, BF16),
            jax.ShapeDtypeStruct((OWN, F), F32),
            jax.ShapeDtypeStruct((OWN, F), F32),
            jax.ShapeDtypeStruct((OWN, F), F32),
        ),
        in_specs=[pl.BlockSpec(memory_space=pltpu.VMEM)] + [pl.BlockSpec(memory_space=pltpu.HBM)] * 4,
        out_specs=(pl.BlockSpec(memory_space=pl.ANY),) * 4,
        scratch_shapes=[
            vmem(shape3, BF16),
            vmem(shape3, BF16),
            vmem(shape3, BF16),
            vmem((2 * DP, R, 128), F32),
            vmem((DP, R, 128), F32),
            vmem((DP, R, 128), F32),
            vmem((DP, R, 128), F32),
            vmem((ZN, 4, 128), F32),
            vmem((ZN, 4, 128), F32),
            vmem((ZN, 4, 128), F32),
            vmem((2 * DP, R, 128), F32),
            vmem((CHUNKS, 3, R, ROWS), BF16),
            vmem((CHUNKS, ROWS, 128), BF16),
            vmem((DP, 2, COLS), F32),
            vmem((DP, 2, COLS), F32),
            vmem((DP, 2, COLS), F32),
            vmem((SH, R, COLS), F32),
            vmem((OWN, F), F32),
            vmem((OWN, F), F32),
            vmem((OWN, F), F32),
            vmem((OWN, F), F32),
            vmem((OWN, F), F32),
            vmem((OWN, F), F32),
            dma((CHUNKS,)), dma((CHUNKS,)), dma((2,)),
            dma((4,)), dma((4,)),
            dma((DP,)), dma((DP,)),
            dma((ZN,)), dma((ZN,)),
            dma((ZN,)), dma((ZN,)),
            dma((DP,)), dma((DP,)),
            dma((DP,)), dma((DP,)),
            dma((DP,)), dma((DP,)),
            dma((DP,)), dma((DP,)),
            dma((ZN,)), dma((ZN,)),
            dma((ZN,)), dma((ZN,)),
            dma((CHUNKS,)), dma((3,)),
        ],
        compiler_params=pltpu.CompilerParams(
            collective_id=0, has_side_effects=True, vmem_limit_bytes=28 * 1024 * 1024
        ),
    )(
        right_init.T,
        gradient.reshape(shape3),
        error_buffer.reshape(shape3),
        first_moment,
        second_moment,
    )
    return (err.reshape(1, D, COLS), first, second, direction)


def solution(mesh):
    return jax.shard_map(
        local,
        mesh=mesh,
        in_specs=(
            P("dp", None, "shard"),
            P("dp", None, "shard"),
            P("shard", None),
            P(("dp", "shard"), None),
            P(("dp", "shard"), None),
        ),
        out_specs=(
            P("dp", None, "shard"),
            P(("dp", "shard"), None),
            P(("dp", "shard"), None),
            P(("dp", "shard"), None),
        ),
        check_vma=False,
    )
```

```python
import jax
import jax.numpy as jnp
from jax import lax
from jax.experimental import pallas as pl
from jax.experimental.pallas import tpu as pltpu
from jax.sharding import PartitionSpec as P

D = 4096
F = 6144
R = 32
DP = 16
SH = 16
ZN = 8
CHUNKS = 8
ROWS = D // CHUNKS
COLS = F // SH
OWN = D // (DP * SH)

CLIP_LEVEL = 0.9
BETA_ONE = 0.9
BETA_TWO = 0.95
EPSILON = 1e-08

MESH = pl.DeviceIdType.MESH
F32 = jnp.float32
BF16 = jnp.bfloat16
NT = (((1,), (1,)), ((), ()))
NN = (((1,), (0,)), ((), ()))


def mm(a, b, dims):
    return lax.dot_general(a, b, dims, preferred_element_type=F32)


def split(x):
    high = x.astype(BF16)
    rest = x - high.astype(F32)
    mid = rest.astype(BF16)
    low = (rest - mid.astype(F32)).astype(BF16)
    return high, mid, low


def fold(full, n):
    rows = sum(full[R * a : R * (a + 1)] for a in range(n))
    return sum(rows[:, R * a : R * (a + 1)] for a in range(n))


def triangular_inverse(gram_matrix):
    row = lax.broadcasted_iota(jnp.int32, (R, R), 0)
    col = lax.broadcasted_iota(jnp.int32, (R, R), 1)
    eye = row == col
    trace = jnp.sum(jnp.where(eye, gram_matrix, 0.0), keepdims=True)
    shifted = gram_matrix + jnp.where(eye, 1e-06 * trace / R, 0.0)
    work = jnp.concatenate([shifted, jnp.where(eye, 1.0, 0.0)], axis=1)
    wide_row = lax.broadcasted_iota(jnp.int32, (R, 2 * R), 0)
    wide_col = lax.broadcasted_iota(jnp.int32, (R, 2 * R), 1)
    for k in range(R - 1):
        column = jnp.broadcast_to(work[:, k : k + 1], (R, 2 * R))
        pivot = column[k : k + 1]
        line = work[k : k + 1] * (1.0 / pivot)
        work = work - jnp.where(wide_row > k, column, 0.0) * line
    diagonal = jnp.sum(jnp.where(wide_row == wide_col, work, 0.0), axis=1, keepdims=True)
    return work[:, R : 2 * R] * lax.rsqrt(diagonal)


def kernel(
    right_hbm, grad_hbm, errb_hbm,
    err_ref, scaled_ref,
    right_buf, grad_buf, errb_buf, merged, part, core_in, half, dp_in, z_in, left_raw,
    left_split, left_stack, right_out, right_in, right_all, right_raw, blocks,
    load_g, load_e, load_m,
    s_core, r_core, s_dp, r_dp, s_z, r_z, s_dpa, r_dpa, s_ca, r_ca,
    s_rr, r_rr, s_ra, r_ra, s_bz, r_bz, s_bc, r_bc,
):
    i = lax.axis_index("dp")
    j = lax.axis_index("shard")
    x, y = i // 4, i % 4
    z, c = j // 2, j % 2
    other = j + 1 - 2 * c

    def dp_peer(d):
        return ((x + d // 4) % 4) * 4 + (y + d % 4) % 4

    def z_peer(d):
        return (z + d) % ZN

    def hops(d):
        return min(d // 4, 4 - d // 4) + min(d % 4, 4 - d % 4)

    dp_near = sorted(range(1, DP), key=hops)
    dp_far = dp_near[::-1]
    z_near = sorted(range(1, ZN), key=lambda d: min(d, ZN - d))
    z_far = z_near[::-1]

    def remote(src, dst, ss, rs, dp, sh):
        return pltpu.make_async_remote_copy(
            src_ref=src, dst_ref=dst, send_sem=ss, recv_sem=rs, device_id=(dp, sh), device_id_type=MESH
        )

    sends = []
    loads = []

    def send(*args):
        copy = remote(*args)
        copy.start()
        sends.append(copy)

    def finish():
        for copy in sends:
            copy.wait_send()

    barrier = pltpu.get_barrier_semaphore()
    for d in dp_far:
        pl.semaphore_signal(barrier, inc=1, device_id=(dp_peer(d), j), device_id_type=MESH)
    for d in z_far:
        pl.semaphore_signal(barrier, inc=1, device_id=(i, 2 * z_peer(d) + c), device_id_type=MESH)
    pl.semaphore_signal(barrier, inc=1, device_id=(i, other), device_id_type=MESH)
    load_right = pltpu.make_async_copy(right_hbm, right_buf, load_m)
    load_right.start()
    for k in range(CHUNKS):
        a = pltpu.make_async_copy(grad_hbm.at[k], grad_buf.at[k], load_g.at[k])
        b = pltpu.make_async_copy(errb_hbm.at[k], errb_buf.at[k], load_e.at[k])
        a.start()
        b.start()
        loads.append((a, b))

    load_right.wait()
    right_low = right_buf[...].astype(BF16)
    for k in range(CHUNKS):
        for copy in loads[k]:
            copy.wait()
        total = (grad_buf[k].astype(F32) + errb_buf[k].astype(F32)).astype(BF16)
        merged[4 * k : 4 * (k + 1)] = total.reshape(4, 128, COLS)
        product = mm(right_low, total, NT)
        for t in range(4):
            part[4 * k + t] = product[:, 128 * t : 128 * (t + 1)]

    pl.semaphore_wait(barrier, DP - 1 + ZN - 1 + 1)
    for k in range(4):
        send(part.at[pl.ds(DP * (1 - c) + 4 * k, 4)], core_in.at[pl.ds(4 * k, 4)], s_core.at[k], r_core.at[k], i, other)
    for k in range(4):
        remote(
            part.at[pl.ds(DP * c + 4 * k, 4)], core_in.at[pl.ds(4 * k, 4)], s_core.at[k], r_core.at[k], i, other
        ).wait_recv()
        for t in range(4 * k, 4 * k + 4):
            half[t] = part[DP * c + t] + core_in[t]
    for d in dp_far:
        p = dp_peer(d)
        send(half.at[p], dp_in.at[i], s_dp.at[d], r_dp.at[i], p, j)
    dp_in[i] = half[i]
    for d in dp_near:
        p = dp_peer(d)
        remote(half.at[p], dp_in.at[p], s_dp.at[d], r_dp.at[p], p, j).wait_recv()
    total = dp_in[0]
    for p in range(1, DP):
        total = total + dp_in[p]
    z_in[z] = total
    for d in z_far:
        p = z_peer(d)
        send(z_in.at[z], z_in.at[z], s_z.at[d], r_z.at[z], i, 2 * p + c)
    for d in z_near:
        p = z_peer(d)
        remote(z_in.at[p], z_in.at[p], s_z.at[d], r_z.at[p], i, 2 * p + c).wait_recv()
    total = z_in[0]
    for p in range(1, ZN):
        total = total + z_in[p]
    mine = DP * c + i
    left_raw[mine] = total * (1.0 / DP)
    for d in dp_far:
        send(left_raw.at[mine], left_raw.at[mine], s_dpa.at[d], r_dpa.at[i], dp_peer(d), j)
    send(left_raw.at[mine], left_raw.at[mine], s_ca.at[i], r_ca.at[i], i, other)
    for d in dp_near:
        p = dp_peer(d)
        q = DP * c + p
        remote(left_raw.at[q], left_raw.at[q], s_dpa.at[d], r_dpa.at[p], p, j).wait_recv()
        send(left_raw.at[q], left_raw.at[q], s_ca.at[p], r_ca.at[p], i, other)
    gram_sum = jnp.zeros((3 * R, 3 * R), F32)
    right_sum = jnp.zeros((3 * R, COLS), F32)
    for k in range(CHUNKS):
        if k < 4:
            first = DP * c + 4 * k
        else:
            first = DP * (1 - c) + 4 * (k - 4)
            for p in range(4 * (k - 4), 4 * (k - 3)):
                q = DP * (1 - c) + p
                remote(left_raw.at[q], left_raw.at[q], s_ca.at[p], r_ca.at[p], i, other).wait_recv()
        wide = jnp.concatenate([left_raw[first + t] for t in range(4)], axis=1)
        stack = jnp.concatenate(split(wide), axis=0)
        left_split[first // 4] = stack
        gram_sum = gram_sum + mm(stack, stack, NT)
        right_sum = right_sum + mm(stack, merged[pl.ds(first, 4)].reshape(ROWS, COLS), NN)
    right_part = right_sum[:R] + right_sum[R : 2 * R] + right_sum[2 * R :]
    for p in range(DP):
        right_out[p] = right_part[2 * p : 2 * p + 2]
    for d in dp_far:
        p = dp_peer(d)
        send(right_out.at[p], right_in.at[i], s_rr.at[d], r_rr.at[i], p, j)
    right_in[i] = right_out[i]
    inverse = split(triangular_inverse(fold(gram_sum, 3)))
    inverse = jnp.concatenate([jnp.concatenate([t] * 3, axis=1) for t in inverse], axis=0)
    for d in dp_near:
        p = dp_peer(d)
        remote(right_out.at[p], right_in.at[p], s_rr.at[d], r_rr.at[p], p, j).wait_recv()
    total = right_in[0]
    for p in range(1, DP):
        total = total + right_in[p]
    right_all[i] = total * (1.0 / DP)
    for d in dp_far:
        send(right_all.at[i], right_all.at[i], s_ra.at[d], r_ra.at[i], dp_peer(d), j)
    ortho_sum = jnp.zeros((2 * R, 2 * R), F32)
    for k in range(CHUNKS):
        wide = mm(inverse, left_split[k], NN)
        high, mid, _ = split(wide[:R] + wide[R : 2 * R] + wide[2 * R :])
        stack = jnp.concatenate([high, mid], axis=0)
        ortho_sum = ortho_sum + mm(stack, stack, NT)
        left_stack[32 * k : 32 * (k + 1)] = jnp.concatenate([high, high, mid, mid], axis=0).T.reshape(32, OWN, 128)
    ortho_gram = fold(ortho_sum, 2)
    for d in dp_near:
        p = dp_peer(d)
        remote(right_all.at[p], right_all.at[p], s_ra.at[d], r_ra.at[p], p, j).wait_recv()
    for p in range(DP):
        right_raw[2 * p : 2 * p + 2] = right_all[p]
    wide = mm(inverse, jnp.concatenate(split(right_raw[...]), axis=0), NN)
    blocks[j] = wide[:R] + wide[R : 2 * R] + wide[2 * R :]
    for d in z_far:
        send(blocks.at[j], blocks.at[j], s_bz.at[d], r_bz.at[z], i, 2 * z_peer(d) + c)
    send(blocks.at[j], blocks.at[j], s_bc.at[z], r_bc.at[z], i, other)
    own = left_stack[DP * i + j]

    def stacked(block):
        high, mid, _ = split(block)
        return jnp.concatenate([high, mid, high, mid], axis=0)

    mine_stack = stacked(blocks[j])
    for k in range(CHUNKS):
        rows = left_stack[32 * k : 32 * (k + 1)].reshape(ROWS, 128)
        whole = merged[4 * k : 4 * (k + 1)].reshape(ROWS, COLS)
        err_ref[k] = (whole.astype(F32) - mm(rows, mine_stack, NN)).astype(BF16)
    for d in z_near:
        p = z_peer(d)
        q = 2 * p + c
        remote(blocks.at[q], blocks.at[q], s_bz.at[d], r_bz.at[p], i, q).wait_recv()
        send(blocks.at[q], blocks.at[q], s_bc.at[p], r_bc.at[p], i, other)
    for p in range(ZN):
        q = 2 * p + 1 - c
        remote(blocks.at[q], blocks.at[q], s_bc.at[p], r_bc.at[p], i, other).wait_recv()
    square = jnp.zeros((2 * R, 2 * R), F32)
    rows = []
    for q in range(SH):
        stack = stacked(blocks[q])
        square = square + mm(stack[: 2 * R], stack[: 2 * R], NT)
        rows.append(mm(own, stack, NN))
    norm = jnp.sqrt(jnp.sum(fold(square, 2) * ortho_gram, keepdims=True))
    clip_level = CLIP_LEVEL * (float(R * (D + F)) ** 0.5)
    scale = clip_level / jnp.maximum(norm, clip_level)
    for q in range(SH):
        scaled_ref[:, COLS * q : COLS * (q + 1)] = rows[q] * scale
    finish()


def step_kernel(
    err_ref, scaled_ref, first_ref, second_ref, err_hbm, first_hbm, second_hbm, direction_hbm,
    first_res, second_res, direction_res, out_e, out_m,
):
    outs = [pltpu.make_async_copy(err_ref, err_hbm, out_e)]
    outs[0].start()
    pieces = 4
    width = F // pieces
    for q in range(pieces):
        lanes = pl.ds(width * q, width)
        scaled = scaled_ref[:, lanes]
        first = BETA_ONE * first_ref[:, lanes] + (1.0 - BETA_ONE) * scaled
        second = BETA_TWO * second_ref[:, lanes] + (1.0 - BETA_TWO) * scaled * scaled
        first_res[:, lanes] = first
        second_res[:, lanes] = second
        direction_res[:, lanes] = first / (jnp.sqrt(second) + EPSILON)
        for n, (res, hbm) in enumerate(
            ((first_res, first_hbm), (second_res, second_hbm), (direction_res, direction_hbm))
        ):
            copy = pltpu.make_async_copy(res.at[:, lanes], hbm.at[:, lanes], out_m.at[n, q])
            copy.start()
            outs.append(copy)
    for copy in outs:
        copy.wait()


def local(gradient, error_buffer, right_init, first_moment, second_moment):
    shape3 = (CHUNKS, ROWS, COLS)
    dma = pltpu.SemaphoreType.DMA
    vmem = pltpu.VMEM
    err, scaled = pl.pallas_call(
        kernel,
        out_shape=(jax.ShapeDtypeStruct(shape3, BF16), jax.ShapeDtypeStruct((OWN, F), F32)),
        in_specs=[pl.BlockSpec(memory_space=pltpu.HBM)] * 3,
        out_specs=(pl.BlockSpec(memory_space=pltpu.VMEM),) * 2,
        scratch_shapes=[
            vmem((R, COLS), F32),
            vmem(shape3, BF16),
            vmem(shape3, BF16),
            vmem((2 * DP, 128, COLS), BF16),
            vmem((2 * DP, R, 128), F32),
            vmem((DP, R, 128), F32),
            vmem((DP, R, 128), F32),
            vmem((DP, R, 128), F32),
            vmem((ZN, R, 128), F32),
            vmem((2 * DP, R, 128), F32),
            vmem((CHUNKS, 3 * R, ROWS), BF16),
            vmem((DP * SH, OWN, 128), BF16),
            vmem((DP, 2, COLS), F32),
            vmem((DP, 2, COLS), F32),
            vmem((DP, 2, COLS), F32),
            vmem((R, COLS), F32),
            vmem((SH, R, COLS), F32),
            dma((CHUNKS,)), dma((CHUNKS,)), dma(()),
            dma((4,)), dma((4,)),
            dma((DP,)), dma((DP,)),
            dma((ZN,)), dma((ZN,)),
            dma((DP,)), dma((DP,)),
            dma((DP,)), dma((DP,)),
            dma((DP,)), dma((DP,)),
            dma((DP,)), dma((DP,)),
            dma((ZN,)), dma((ZN,)),
            dma((ZN,)), dma((ZN,)),
        ],
        compiler_params=pltpu.CompilerParams(
            collective_id=0, has_side_effects=True, vmem_limit_bytes=28 * 1024 * 1024
        ),
    )(
        *(
            pltpu.with_memory_space_constraint(t, pltpu.HBM)
            for t in (right_init.T, gradient.reshape(shape3), error_buffer.reshape(shape3))
        )
    )
    own = jax.ShapeDtypeStruct((OWN, F), F32)
    err, first, second, direction = pl.pallas_call(
        step_kernel,
        out_shape=(jax.ShapeDtypeStruct(shape3, BF16), own, own, own),
        in_specs=[pl.BlockSpec(memory_space=pl.ANY)] + [pl.BlockSpec(memory_space=pltpu.VMEM)] * 3,
        out_specs=(pl.BlockSpec(memory_space=pltpu.HBM),) * 4,
        scratch_shapes=[
            vmem((OWN, F), F32), vmem((OWN, F), F32), vmem((OWN, F), F32),
            dma(()), dma((3, 4)),
        ],
        compiler_params=pltpu.CompilerParams(vmem_limit_bytes=4 * 1024 * 1024),
    )(err, scaled, first_moment, second_moment)
    return (err.reshape(1, D, COLS), first, second, direction)


def solution(mesh):
    return jax.shard_map(
        local,
        mesh=mesh,
        in_specs=(
            P("dp", None, "shard"),
            P("dp", None, "shard"),
            P("shard", None),
            P(("dp", "shard"), None),
            P(("dp", "shard"), None),
        ),
        out_specs=(
            P("dp", None, "shard"),
            P(("dp", "shard"), None),
            P(("dp", "shard"), None),
            P(("dp", "shard"), None),
        ),
        check_vma=False,
    )
```

```python
import jax
import jax.numpy as jnp
from jax import lax
from jax.experimental import pallas as pl
from jax.experimental.pallas import tpu as pltpu
from jax.sharding import PartitionSpec as P

D = 4096
F = 6144
R = 32
DP = 16
SH = 16
ZN = 8
CHUNKS = 8
ROWS = D // CHUNKS
COLS = F // SH
OWN = D // (DP * SH)
PIECES = (R // 8) * (COLS // 128)
AHEAD = 3

CLIP_LEVEL = 0.9
BETA_ONE = 0.9
BETA_TWO = 0.95
EPSILON = 1e-08

MESH = pl.DeviceIdType.MESH
F32 = jnp.float32
BF16 = jnp.bfloat16
NT = (((1,), (1,)), ((), ()))
NN = (((1,), (0,)), ((), ()))


def mm(a, b, dims):
    return lax.dot_general(a, b, dims, preferred_element_type=F32)


def split(x):
    high = x.astype(BF16)
    rest = x - high.astype(F32)
    mid = rest.astype(BF16)
    low = (rest - mid.astype(F32)).astype(BF16)
    return high, mid, low


def fold(full, n):
    rows = sum(full[R * a : R * (a + 1)] for a in range(n))
    return sum(rows[:, R * a : R * (a + 1)] for a in range(n))


def triangular_inverse(gram_matrix):
    row = lax.broadcasted_iota(jnp.int32, (R, R), 0)
    col = lax.broadcasted_iota(jnp.int32, (R, R), 1)
    eye = row == col
    trace = jnp.sum(jnp.where(eye, gram_matrix, 0.0), keepdims=True)
    shifted = gram_matrix + jnp.where(eye, 1e-06 * trace / R, 0.0)
    work = jnp.concatenate([shifted, jnp.where(eye, 1.0, 0.0)], axis=1)
    wide_row = lax.broadcasted_iota(jnp.int32, (R, 2 * R), 0)
    wide_col = lax.broadcasted_iota(jnp.int32, (R, 2 * R), 1)
    for k in range(R - 1):
        column = jnp.broadcast_to(work[:, k : k + 1], (R, 2 * R))
        pivot = column[k : k + 1]
        line = work[k : k + 1] * (1.0 / pivot)
        work = work - jnp.where(wide_row > k, column, 0.0) * line
    diagonal = jnp.sum(jnp.where(wide_row == wide_col, work, 0.0), axis=1, keepdims=True)
    return work[:, R : 2 * R] * lax.rsqrt(diagonal)


def kernel(
    right_hbm, grad_hbm, errb_hbm,
    err_ref, scaled_ref,
    right_buf, grad_buf, errb_buf, merged, part, core_in, half, dp_in, z_in, left_raw,
    left_split, left_stack, right_out, right_in, right_all, planes, owned,
    load_g, load_e, load_m,
    s_core, r_core, s_dp, r_dp, s_z, r_z, s_dpa, r_dpa, s_ca, r_ca,
    s_rr, r_rr, s_ra, r_ra, s_bz, r_bz, s_pl, r_pl, s_bc, r_bc,
):
    i = lax.axis_index("dp")
    j = lax.axis_index("shard")
    x, y = i // 4, i % 4
    z, c = j // 2, j % 2
    other = j + 1 - 2 * c

    def dp_peer(d):
        return ((x + d // 4) % 4) * 4 + (y + d % 4) % 4

    def z_peer(d):
        return (z + d) % ZN

    def hops(d):
        return min(d // 4, 4 - d // 4) + min(d % 4, 4 - d % 4)

    dp_near = sorted(range(1, DP), key=hops)
    dp_far = dp_near[::-1]
    z_near = sorted(range(1, ZN), key=lambda d: min(d, ZN - d))
    z_far = z_near[::-1]

    def remote(src, dst, ss, rs, dp, sh):
        return pltpu.make_async_remote_copy(
            src_ref=src, dst_ref=dst, send_sem=ss, recv_sem=rs, device_id=(dp, sh), device_id_type=MESH
        )

    sends = []
    loads = []

    def send(*args):
        copy = remote(*args)
        copy.start()
        sends.append(copy)

    def finish():
        for copy in sends:
            copy.wait_send()

    barrier = pltpu.get_barrier_semaphore()
    for d in dp_far:
        pl.semaphore_signal(barrier, inc=1, device_id=(dp_peer(d), j), device_id_type=MESH)
    for d in z_far:
        pl.semaphore_signal(barrier, inc=1, device_id=(i, 2 * z_peer(d) + c), device_id_type=MESH)
    pl.semaphore_signal(barrier, inc=1, device_id=(i, other), device_id_type=MESH)
    load_right = pltpu.make_async_copy(right_hbm, right_buf, load_m)
    load_right.start()

    def load(k):
        a = pltpu.make_async_copy(grad_hbm.at[k], grad_buf.at[k], load_g.at[k])
        b = pltpu.make_async_copy(errb_hbm.at[k], errb_buf.at[k], load_e.at[k])
        a.start()
        b.start()
        loads.append((a, b))

    for k in range(AHEAD):
        load(k)

    load_right.wait()
    right_low = right_buf[...].astype(BF16)
    for k in range(CHUNKS):
        for copy in loads[k]:
            copy.wait()
        if k + AHEAD < CHUNKS:
            load(k + AHEAD)
        total = (grad_buf[k].astype(F32) + errb_buf[k].astype(F32)).astype(BF16)
        merged[4 * k : 4 * (k + 1)] = total.reshape(4, 128, COLS)
        product = mm(right_low, total, NT)
        for t in range(4):
            part[4 * k + t] = product[:, 128 * t : 128 * (t + 1)]

    pl.semaphore_wait(barrier, DP - 1 + ZN - 1 + 1)
    for k in range(4):
        send(part.at[pl.ds(DP * (1 - c) + 4 * k, 4)], core_in.at[pl.ds(4 * k, 4)], s_core.at[k], r_core.at[k], i, other)
    for k in range(4):
        remote(
            part.at[pl.ds(DP * c + 4 * k, 4)], core_in.at[pl.ds(4 * k, 4)], s_core.at[k], r_core.at[k], i, other
        ).wait_recv()
        for t in range(4 * k, 4 * k + 4):
            half[t] = part[DP * c + t] + core_in[t]
    for d in dp_far:
        p = dp_peer(d)
        send(half.at[p], dp_in.at[i], s_dp.at[d], r_dp.at[i], p, j)
    dp_in[i] = half[i]
    for d in dp_near:
        p = dp_peer(d)
        remote(half.at[p], dp_in.at[p], s_dp.at[d], r_dp.at[p], p, j).wait_recv()
    total = dp_in[0]
    for p in range(1, DP):
        total = total + dp_in[p]
    z_in[z] = total
    for d in z_far:
        p = z_peer(d)
        send(z_in.at[z], z_in.at[z], s_z.at[d], r_z.at[z], i, 2 * p + c)
    for d in z_near:
        p = z_peer(d)
        remote(z_in.at[p], z_in.at[p], s_z.at[d], r_z.at[p], i, 2 * p + c).wait_recv()
    total = z_in[0]
    for p in range(1, ZN):
        total = total + z_in[p]
    mine = DP * c + i
    left_raw[mine] = total * (1.0 / DP)
    for d in dp_far:
        send(left_raw.at[mine], left_raw.at[mine], s_dpa.at[d], r_dpa.at[i], dp_peer(d), j)
    send(left_raw.at[mine], left_raw.at[mine], s_ca.at[i], r_ca.at[i], i, other)
    for d in dp_near:
        p = dp_peer(d)
        q = DP * c + p
        remote(left_raw.at[q], left_raw.at[q], s_dpa.at[d], r_dpa.at[p], p, j).wait_recv()
        send(left_raw.at[q], left_raw.at[q], s_ca.at[p], r_ca.at[p], i, other)
    gram_sum = jnp.zeros((3 * R, 3 * R), F32)
    right_sum = jnp.zeros((3 * R, COLS), F32)
    for k in range(CHUNKS):
        if k < 4:
            first = DP * c + 4 * k
        else:
            first = DP * (1 - c) + 4 * (k - 4)
            for p in range(4 * (k - 4), 4 * (k - 3)):
                q = DP * (1 - c) + p
                remote(left_raw.at[q], left_raw.at[q], s_ca.at[p], r_ca.at[p], i, other).wait_recv()
        wide = jnp.concatenate([left_raw[first + t] for t in range(4)], axis=1)
        stack = jnp.concatenate(split(wide), axis=0)
        left_split[first // 4] = stack
        gram_sum = gram_sum + mm(stack, stack, NT)
        right_sum = right_sum + mm(stack, merged[pl.ds(first, 4)].reshape(ROWS, COLS), NN)
    right_part = right_sum[:R] + right_sum[R : 2 * R] + right_sum[2 * R :]
    for p in range(DP):
        g, t = (p % PIECES) // 3, p % 3
        right_out[p] = right_part[8 * g : 8 * (g + 1), 128 * t : 128 * (t + 1)]
    for d in dp_far:
        p = dp_peer(d)
        send(right_out.at[p], right_in.at[i], s_rr.at[d], r_rr.at[i], p, j)
    right_in[i] = right_out[i]
    inverse = split(triangular_inverse(fold(gram_sum, 3)))
    inverse = jnp.concatenate([jnp.concatenate([t] * 3, axis=1) for t in inverse], axis=0)

    def orthonormal(stack):
        wide = mm(inverse, stack, NN)
        return wide[:R] + wide[R : 2 * R] + wide[2 * R :]

    for d in dp_near:
        p = dp_peer(d)
        remote(right_out.at[p], right_in.at[p], s_rr.at[d], r_rr.at[p], p, j).wait_recv()
    total = right_in[0]
    for p in range(1, DP):
        total = total + right_in[p]
    total = total * (1.0 / DP)
    right_all[i] = total
    planes[c, i, z] = total
    for d in z_far:
        send(planes.at[c, i, z], planes.at[c, i, z], s_bz.at[d], r_bz.at[z], i, 2 * z_peer(d) + c)
    for d in dp_far:
        send(right_all.at[i], right_all.at[i], s_ra.at[d], r_ra.at[i], dp_peer(d), j)
    ortho_sum = jnp.zeros((2 * R, 2 * R), F32)
    for k in range(CHUNKS):
        high, mid, _ = split(orthonormal(left_split[k]))
        stack = jnp.concatenate([high, mid], axis=0)
        ortho_sum = ortho_sum + mm(stack, stack, NT)
        left_stack[32 * k : 32 * (k + 1)] = jnp.concatenate([high, high, mid, mid], axis=0).T.reshape(32, OWN, 128)
    ortho_gram = fold(ortho_sum, 2)
    for d in z_near:
        p = z_peer(d)
        remote(planes.at[c, i, p], planes.at[c, i, p], s_bz.at[d], r_bz.at[p], i, 2 * p + c).wait_recv()
    def spread():
        for d in dp_far:
            yield remote(planes.at[c, i], planes.at[c, i], s_pl.at[d], r_pl.at[i], dp_peer(d), j)
        yield remote(planes.at[c, i], planes.at[c, i], s_bc.at[i], r_bc.at[i], i, other)

    @pl.when(i < PIECES)
    def _():
        for copy in spread():
            copy.start()

    for d in dp_near:
        p = dp_peer(d)
        remote(right_all.at[p], right_all.at[p], s_ra.at[d], r_ra.at[p], p, j).wait_recv()

    def stacked(pieces):
        raw = jnp.concatenate(
            [jnp.concatenate([pieces[3 * g + t] for t in range(3)], axis=1) for g in range(R // 8)], axis=0
        )
        high, mid, _ = split(orthonormal(jnp.concatenate(split(raw), axis=0)))
        return jnp.concatenate([high, mid, high, mid], axis=0)

    mine_stack = stacked([right_all[p] for p in range(PIECES)])
    own = left_stack[DP * i + j]
    for k in range(CHUNKS):
        rows = left_stack[32 * k : 32 * (k + 1)].reshape(ROWS, 128)
        whole = merged[4 * k : 4 * (k + 1)].reshape(ROWS, COLS)
        err_ref[k] = (whole.astype(F32) - mm(rows, mine_stack, NN)).astype(BF16)

    def relay(d):
        p = dp_peer(d)
        return p, remote(planes.at[c, p], planes.at[c, p], s_bc.at[p], r_bc.at[p], i, other)

    for d in dp_near:
        p, copy = relay(d)

        @pl.when(p < PIECES)
        def _():
            remote(planes.at[c, p], planes.at[c, p], s_pl.at[d], r_pl.at[p], p, j).wait_recv()
            copy.start()

    square = jnp.zeros((2 * R, 2 * R), F32)
    for n in range(2):
        core = c if n == 0 else 1 - c
        if n == 1:
            for p in range(PIECES):
                remote(planes.at[core, p], planes.at[core, p], s_bc.at[p], r_bc.at[p], i, other).wait_recv()
        for k in range(ZN):
            stack = stacked([planes[core, p, k] for p in range(PIECES)])
            square = square + mm(stack[: 2 * R], stack[: 2 * R], NT)
            owned[2 * k + core] = mm(own, stack, NN)
    norm = jnp.sqrt(jnp.sum(fold(square, 2) * ortho_gram, keepdims=True))
    clip_level = CLIP_LEVEL * (float(R * (D + F)) ** 0.5)
    scale = clip_level / jnp.maximum(norm, clip_level)
    for q in range(SH):
        scaled_ref[:, COLS * q : COLS * (q + 1)] = owned[q] * scale
    finish()
    for d in dp_near:
        p, copy = relay(d)

        @pl.when(p < PIECES)
        def _():
            copy.wait_send()

    @pl.when(i < PIECES)
    def _():
        for copy in spread():
            copy.wait_send()


def step_kernel(
    err_ref, scaled_ref, first_ref, second_ref, err_hbm, first_hbm, second_hbm, direction_hbm,
    first_res, second_res, direction_res, out_e, out_m,
):
    outs = []
    for k in range(4):
        chunks = pl.ds(k * CHUNKS // 4, CHUNKS // 4)
        copy = pltpu.make_async_copy(err_ref.at[chunks], err_hbm.at[chunks], out_e.at[k])
        copy.start()
        outs.append(copy)
    pieces = 4
    width = F // pieces
    for q in range(pieces):
        lanes = pl.ds(width * q, width)
        scaled = scaled_ref[:, lanes]
        first = BETA_ONE * first_ref[:, lanes] + (1.0 - BETA_ONE) * scaled
        second = BETA_TWO * second_ref[:, lanes] + (1.0 - BETA_TWO) * scaled * scaled
        first_res[:, lanes] = first
        second_res[:, lanes] = second
        direction_res[:, lanes] = first / (jnp.sqrt(second) + EPSILON)
        for n, (res, hbm) in enumerate(
            ((first_res, first_hbm), (second_res, second_hbm), (direction_res, direction_hbm))
        ):
            copy = pltpu.make_async_copy(res.at[:, lanes], hbm.at[:, lanes], out_m.at[n, q])
            copy.start()
            outs.append(copy)
    for copy in outs:
        copy.wait()


def local(gradient, error_buffer, right_init, first_moment, second_moment):
    shape3 = (CHUNKS, ROWS, COLS)
    dma = pltpu.SemaphoreType.DMA
    vmem = pltpu.VMEM
    err, scaled = pl.pallas_call(
        kernel,
        out_shape=(jax.ShapeDtypeStruct(shape3, BF16), jax.ShapeDtypeStruct((OWN, F), F32)),
        in_specs=[pl.BlockSpec(memory_space=pltpu.HBM)] * 3,
        out_specs=(pl.BlockSpec(memory_space=pltpu.VMEM),) * 2,
        scratch_shapes=[
            vmem((R, COLS), F32),
            vmem(shape3, BF16),
            vmem(shape3, BF16),
            vmem((2 * DP, 128, COLS), BF16),
            vmem((2 * DP, R, 128), F32),
            vmem((DP, R, 128), F32),
            vmem((DP, R, 128), F32),
            vmem((DP, R, 128), F32),
            vmem((ZN, R, 128), F32),
            vmem((2 * DP, R, 128), F32),
            vmem((CHUNKS, 3 * R, ROWS), BF16),
            vmem((DP * SH, OWN, 128), BF16),
            vmem((DP, 8, 128), F32),
            vmem((DP, 8, 128), F32),
            vmem((DP, 8, 128), F32),
            vmem((2, DP, ZN, 8, 128), F32),
            vmem((SH, OWN, COLS), F32),
            dma((CHUNKS,)), dma((CHUNKS,)), dma(()),
            dma((4,)), dma((4,)),
            dma((DP,)), dma((DP,)),
            dma((ZN,)), dma((ZN,)),
            dma((DP,)), dma((DP,)),
            dma((DP,)), dma((DP,)),
            dma((DP,)), dma((DP,)),
            dma((DP,)), dma((DP,)),
            dma((ZN,)), dma((ZN,)),
            dma((DP,)), dma((DP,)),
            dma((DP,)), dma((DP,)),
        ],
        compiler_params=pltpu.CompilerParams(
            collective_id=0, has_side_effects=True, vmem_limit_bytes=28 * 1024 * 1024
        ),
    )(
        *(
            pltpu.with_memory_space_constraint(t, pltpu.HBM)
            for t in (right_init.T, gradient.reshape(shape3), error_buffer.reshape(shape3))
        )
    )
    own = jax.ShapeDtypeStruct((OWN, F), F32)
    err, first, second, direction = pl.pallas_call(
        step_kernel,
        out_shape=(jax.ShapeDtypeStruct(shape3, BF16), own, own, own),
        in_specs=[pl.BlockSpec(memory_space=pl.ANY)] + [pl.BlockSpec(memory_space=pltpu.VMEM)] * 3,
        out_specs=(pl.BlockSpec(memory_space=pltpu.HBM),) * 4,
        scratch_shapes=[
            vmem((OWN, F), F32), vmem((OWN, F), F32), vmem((OWN, F), F32),
            dma((4,)), dma((3, 4)),
        ],
        compiler_params=pltpu.CompilerParams(vmem_limit_bytes=4 * 1024 * 1024),
    )(err, scaled, first_moment, second_moment)
    return (err.reshape(1, D, COLS), first, second, direction)


def solution(mesh):
    return jax.shard_map(
        local,
        mesh=mesh,
        in_specs=(
            P("dp", None, "shard"),
            P("dp", None, "shard"),
            P("shard", None),
            P(("dp", "shard"), None),
            P(("dp", "shard"), None),
        ),
        out_specs=(
            P("dp", None, "shard"),
            P(("dp", "shard"), None),
            P(("dp", "shard"), None),
            P(("dp", "shard"), None),
        ),
        check_vma=False,
    )
```

```python
import jax
import jax.numpy as jnp
from jax import lax
from jax.experimental import pallas as pl
from jax.experimental.pallas import tpu as pltpu
from jax.sharding import PartitionSpec as P

D = 4096
F = 6144
R = 32
DP = 16
SH = 16
ZN = 8
CHUNKS = 8
ROWS = D // CHUNKS
COLS = F // SH
OWN = D // (DP * SH)
PIECES = (R // 8) * (COLS // 128)
AHEAD = 3
PANEL = 8

CLIP_LEVEL = 0.9
BETA_ONE = 0.9
BETA_TWO = 0.95
EPSILON = 1e-08

MESH = pl.DeviceIdType.MESH
F32 = jnp.float32
BF16 = jnp.bfloat16
NT = (((1,), (1,)), ((), ()))
NN = (((1,), (0,)), ((), ()))


def mm(a, b, dims):
    return lax.dot_general(a, b, dims, preferred_element_type=F32)


def split(x):
    high = x.astype(BF16)
    rest = x - high.astype(F32)
    mid = rest.astype(BF16)
    low = (rest - mid.astype(F32)).astype(BF16)
    return high, mid, low


def fold(full, n):
    rows = sum(full[R * a : R * (a + 1)] for a in range(n))
    return sum(rows[:, R * a : R * (a + 1)] for a in range(n))


def fold_lanes(wide):
    return wide[:, :R] + wide[:, R : 2 * R] + wide[:, 2 * R :]


def triangular_inverse(gram_matrix):
    row = lax.broadcasted_iota(jnp.int32, (R, R), 0)
    col = lax.broadcasted_iota(jnp.int32, (R, R), 1)
    eye = row == col
    trace = jnp.sum(jnp.where(eye, gram_matrix, 0.0), keepdims=True)
    shifted = gram_matrix + jnp.where(eye, 1e-06 * trace / R, 0.0)
    work = jnp.concatenate([shifted, jnp.where(eye, 1.0, 0.0)], axis=1)
    wide_row = lax.broadcasted_iota(jnp.int32, (R, 2 * R), 0)
    wide_col = lax.broadcasted_iota(jnp.int32, (R, 2 * R), 1)
    for k in range(0, R, PANEL):
        columns = [jnp.broadcast_to(work[:, k + b : k + b + 1], (R, 2 * R)) for b in range(PANEL)]
        rows = [work[k + b : k + b + 1] for b in range(PANEL)]
        for b in range(PANEL):
            inverse = 1.0 / columns[b][k + b : k + b + 1]
            line = rows[b] * inverse
            below = jnp.where(wide_row > k + b, columns[b], 0.0)
            for a in range(b + 1, PANEL):
                entry = columns[b][k + a : k + a + 1]
                columns[a] = columns[a] - columns[b] * (entry * inverse)
                rows[a] = rows[a] - entry * line
            work = work - below * line
    diagonal = jnp.sum(jnp.where(wide_row == wide_col, work, 0.0), axis=1, keepdims=True)
    return work[:, R : 2 * R] * lax.rsqrt(diagonal)


def kernel(
    right_hbm, grad_hbm, errb_hbm,
    err_ref, scaled_ref,
    right_buf, grad_buf, errb_buf, merged, part, core_in, half, dp_in, z_in, left_raw,
    left_split, left_stack, right_out, right_in, right_all, planes, norms,
    load_g, load_e, load_m,
    s_core, r_core, s_dp, r_dp, s_z, r_z, s_dpa, r_dpa, s_ca, r_ca,
    s_rr, r_rr, s_ra, r_ra, s_bz, r_bz, s_pl, r_pl, s_bc, r_bc, s_nz, r_nz, s_nc, r_nc,
):
    i = lax.axis_index("dp")
    j = lax.axis_index("shard")
    x, y = i // 4, i % 4
    z, c = j // 2, j % 2
    other = j + 1 - 2 * c

    def dp_peer(d):
        return ((x + d // 4) % 4) * 4 + (y + d % 4) % 4

    def z_peer(d):
        return (z + d) % ZN

    def hops(d):
        return min(d // 4, 4 - d // 4) + min(d % 4, 4 - d % 4)

    dp_near = sorted(range(1, DP), key=hops)
    dp_far = dp_near[::-1]
    z_near = sorted(range(1, ZN), key=lambda d: min(d, ZN - d))
    z_far = z_near[::-1]

    def remote(src, dst, ss, rs, dp, sh):
        return pltpu.make_async_remote_copy(
            src_ref=src, dst_ref=dst, send_sem=ss, recv_sem=rs, device_id=(dp, sh), device_id_type=MESH
        )

    sends = []
    loads = []

    def send(*args):
        copy = remote(*args)
        copy.start()
        sends.append(copy)

    def finish():
        for copy in sends:
            copy.wait_send()

    barrier = pltpu.get_barrier_semaphore()
    for d in dp_far:
        pl.semaphore_signal(barrier, inc=1, device_id=(dp_peer(d), j), device_id_type=MESH)
    for d in z_far:
        pl.semaphore_signal(barrier, inc=1, device_id=(i, 2 * z_peer(d) + c), device_id_type=MESH)
    pl.semaphore_signal(barrier, inc=1, device_id=(i, other), device_id_type=MESH)
    load_right = pltpu.make_async_copy(right_hbm, right_buf, load_m)
    load_right.start()

    def load(k):
        a = pltpu.make_async_copy(grad_hbm.at[k], grad_buf.at[k], load_g.at[k])
        b = pltpu.make_async_copy(errb_hbm.at[k], errb_buf.at[k], load_e.at[k])
        a.start()
        b.start()
        loads.append((a, b))

    for k in range(AHEAD):
        load(k)

    load_right.wait()
    right_low = right_buf[...].astype(BF16)
    for k in range(CHUNKS):
        for copy in loads[k]:
            copy.wait()
        if k + AHEAD < CHUNKS:
            load(k + AHEAD)
        total = (grad_buf[k].astype(F32) + errb_buf[k].astype(F32)).astype(BF16)
        merged[4 * k : 4 * (k + 1)] = total.reshape(4, 128, COLS)
        product = mm(right_low, total, NT)
        for t in range(4):
            part[4 * k + t] = product[:, 128 * t : 128 * (t + 1)]

    pl.semaphore_wait(barrier, DP - 1 + ZN - 1 + 1)
    for k in range(4):
        send(part.at[pl.ds(DP * (1 - c) + 4 * k, 4)], core_in.at[pl.ds(4 * k, 4)], s_core.at[k], r_core.at[k], i, other)
    for k in range(4):
        remote(
            part.at[pl.ds(DP * c + 4 * k, 4)], core_in.at[pl.ds(4 * k, 4)], s_core.at[k], r_core.at[k], i, other
        ).wait_recv()
        for t in range(4 * k, 4 * k + 4):
            half[t] = part[DP * c + t] + core_in[t]
    for d in dp_far:
        p = dp_peer(d)
        send(half.at[p], dp_in.at[i], s_dp.at[d], r_dp.at[i], p, j)
    dp_in[i] = half[i]
    for d in dp_near:
        p = dp_peer(d)
        remote(half.at[p], dp_in.at[p], s_dp.at[d], r_dp.at[p], p, j).wait_recv()
    total = dp_in[0]
    for p in range(1, DP):
        total = total + dp_in[p]
    z_in[z] = total
    for d in z_far:
        p = z_peer(d)
        send(z_in.at[z], z_in.at[z], s_z.at[d], r_z.at[z], i, 2 * p + c)
    for d in z_near:
        p = z_peer(d)
        remote(z_in.at[p], z_in.at[p], s_z.at[d], r_z.at[p], i, 2 * p + c).wait_recv()
    total = z_in[0]
    for p in range(1, ZN):
        total = total + z_in[p]
    mine = DP * c + i
    left_raw[mine] = total * (1.0 / DP)
    for d in dp_far:
        send(left_raw.at[mine], left_raw.at[mine], s_dpa.at[d], r_dpa.at[i], dp_peer(d), j)
    send(left_raw.at[mine], left_raw.at[mine], s_ca.at[i], r_ca.at[i], i, other)

    def accumulate(sums, tiles):
        wide = jnp.concatenate([left_raw[q] for q in tiles], axis=1)
        stack = jnp.concatenate(split(wide), axis=0)
        for n, q in enumerate(tiles):
            left_split[q] = stack[:, 128 * n : 128 * (n + 1)]
        rows = jnp.concatenate([merged[q] for q in tiles], axis=0)
        return sums[0] + mm(stack, stack, NT), sums[1] + mm(stack, rows, NN)

    sums = jnp.zeros((3 * R, 3 * R), F32), jnp.zeros((3 * R, COLS), F32)
    order = [0] + dp_near
    for g in range(4):
        group = order[4 * g : 4 * (g + 1)]
        for d in group:
            p = dp_peer(d)
            q = DP * c + p
            if d:
                remote(left_raw.at[q], left_raw.at[q], s_dpa.at[d], r_dpa.at[p], p, j).wait_recv()
                send(left_raw.at[q], left_raw.at[q], s_ca.at[p], r_ca.at[p], i, other)
        sums = accumulate(sums, [DP * c + dp_peer(d) for d in group])
    for g in range(4):
        group = order[4 * g : 4 * (g + 1)]
        for d in group:
            p = dp_peer(d)
            q = DP * (1 - c) + p
            remote(left_raw.at[q], left_raw.at[q], s_ca.at[p], r_ca.at[p], i, other).wait_recv()
        sums = accumulate(sums, [DP * (1 - c) + dp_peer(d) for d in group])
    gram_sum, right_sum = sums
    right_part = right_sum[:R] + right_sum[R : 2 * R] + right_sum[2 * R :]
    for p in range(DP):
        g, t = (p % PIECES) // 3, p % 3
        right_out[p] = right_part[8 * g : 8 * (g + 1), 128 * t : 128 * (t + 1)]
    for d in dp_far:
        p = dp_peer(d)
        send(right_out.at[p], right_in.at[i], s_rr.at[d], r_rr.at[i], p, j)
    right_in[i] = right_out[i]
    inverse_parts = split(triangular_inverse(fold(gram_sum, 3)))
    inverse = jnp.concatenate([jnp.concatenate([t] * 3, axis=1) for t in inverse_parts], axis=0)

    def orthonormal(stack):
        wide = mm(inverse, stack, NN)
        return wide[:R] + wide[R : 2 * R] + wide[2 * R :]

    for d in dp_near:
        p = dp_peer(d)
        remote(right_out.at[p], right_in.at[p], s_rr.at[d], r_rr.at[p], p, j).wait_recv()
    total = right_in[0]
    for p in range(1, DP):
        total = total + right_in[p]
    total = total * (1.0 / DP)
    right_all[i] = total
    planes[c, i, z] = total
    for d in z_far:
        send(planes.at[c, i, z], planes.at[c, i, z], s_bz.at[d], r_bz.at[z], i, 2 * z_peer(d) + c)
    for d in dp_far:
        send(right_all.at[i], right_all.at[i], s_ra.at[d], r_ra.at[i], dp_peer(d), j)
    ortho_sum = jnp.zeros((2 * R, 2 * R), F32)
    for k in range(CHUNKS):
        wide = jnp.concatenate([left_split[4 * k + t] for t in range(4)], axis=1)
        high, mid, _ = split(orthonormal(wide))
        stack = jnp.concatenate([high, mid], axis=0)
        ortho_sum = ortho_sum + mm(stack, stack, NT)
        left_stack[32 * k : 32 * (k + 1)] = jnp.concatenate([high, high, mid, mid], axis=0).T.reshape(32, OWN, 128)
    ortho_gram = fold(ortho_sum, 2)
    pick = (
        lax.broadcasted_iota(jnp.int32, (OWN, 128), 1)
        == lax.broadcasted_iota(jnp.int32, (OWN, 128), 0) + OWN * (j % 8)
    )
    own = mm(jnp.where(pick, 1.0, 0.0).astype(BF16), left_split[2 * i + j // 8], NT).astype(BF16)
    own = fold_lanes(mm(own, inverse, NT))
    own = mm(
        jnp.concatenate(split(own), axis=1),
        jnp.concatenate([jnp.concatenate([t] * 3, axis=0) for t in inverse_parts], axis=1),
        NN,
    )
    own = fold_lanes(own)
    for d in z_near:
        p = z_peer(d)
        remote(planes.at[c, i, p], planes.at[c, i, p], s_bz.at[d], r_bz.at[p], i, 2 * p + c).wait_recv()
    def spread():
        for d in dp_far:
            yield remote(planes.at[c, i], planes.at[c, i], s_pl.at[d], r_pl.at[i], dp_peer(d), j)
        yield remote(planes.at[c, i], planes.at[c, i], s_bc.at[i], r_bc.at[i], i, other)

    @pl.when(i < PIECES)
    def _():
        for copy in spread():
            copy.start()

    for d in dp_near:
        p = dp_peer(d)
        remote(right_all.at[p], right_all.at[p], s_ra.at[d], r_ra.at[p], p, j).wait_recv()

    def raw_stack(pieces):
        raw = jnp.concatenate(
            [jnp.concatenate([pieces[3 * g + t] for t in range(3)], axis=1) for g in range(R // 8)], axis=0
        )
        return jnp.concatenate(split(raw), axis=0)

    high, mid, _ = split(orthonormal(raw_stack([right_all[p] for p in range(PIECES)])))
    mine_stack = jnp.concatenate([high, mid, high, mid], axis=0)
    square = fold(mm(mine_stack[: 2 * R], mine_stack[: 2 * R], NT), 2)
    norms[c, z] = jnp.broadcast_to(jnp.sum(square * ortho_gram, keepdims=True), (8, 128))
    for d in z_far:
        send(norms.at[c, z], norms.at[c, z], s_nz.at[d], r_nz.at[z], i, 2 * z_peer(d) + c)
    send(norms.at[c, z], norms.at[c, z], s_nc.at[z], r_nc.at[z], i, other)
    for k in range(CHUNKS):
        rows = left_stack[32 * k : 32 * (k + 1)].reshape(ROWS, 128)
        whole = merged[4 * k : 4 * (k + 1)].reshape(ROWS, COLS)
        err_ref[k] = (whole.astype(F32) - mm(rows, mine_stack, NN)).astype(BF16)

    for d in z_near:
        p = z_peer(d)
        remote(norms.at[c, p], norms.at[c, p], s_nz.at[d], r_nz.at[p], i, 2 * p + c).wait_recv()
        send(norms.at[c, p], norms.at[c, p], s_nc.at[p], r_nc.at[p], i, other)
    for p in range(ZN):
        remote(norms.at[1 - c, p], norms.at[1 - c, p], s_nc.at[p], r_nc.at[p], i, other).wait_recv()
    total = norms[0, 0]
    for k in range(1, SH):
        total = total + norms[k // ZN, k % ZN]
    clip_level = CLIP_LEVEL * (float(R * (D + F)) ** 0.5)
    scale = clip_level / jnp.maximum(jnp.sqrt(total[0:1, 0:1]), clip_level)
    own_stack = jnp.concatenate([jnp.concatenate([t] * 3, axis=1) for t in split(own * scale)], axis=0)

    def relay(d):
        p = dp_peer(d)
        return p, remote(planes.at[c, p], planes.at[c, p], s_bc.at[p], r_bc.at[p], i, other)

    for d in dp_near:
        p, copy = relay(d)

        @pl.when(p < PIECES)
        def _():
            remote(planes.at[c, p], planes.at[c, p], s_pl.at[d], r_pl.at[p], p, j).wait_recv()
            copy.start()

    for n in range(2):
        core = c if n == 0 else 1 - c
        if n == 1:
            for p in range(PIECES):
                remote(planes.at[core, p], planes.at[core, p], s_bc.at[p], r_bc.at[p], i, other).wait_recv()
        for k in range(ZN):
            wide = mm(own_stack, raw_stack([planes[core, p, k] for p in range(PIECES)]), NN)
            scaled_ref[2 * k + core] = wide[:OWN] + wide[OWN : 2 * OWN] + wide[2 * OWN :]
    finish()
    for d in dp_near:
        p, copy = relay(d)

        @pl.when(p < PIECES)
        def _():
            copy.wait_send()

    @pl.when(i < PIECES)
    def _():
        for copy in spread():
            copy.wait_send()


def step_kernel(
    err_ref, scaled_ref, first_ref, second_ref, err_hbm, first_hbm, second_hbm, direction_hbm,
    first_res, second_res, direction_res, out_e, out_m,
):
    outs = []
    for k in range(4):
        chunks = pl.ds(k * CHUNKS // 4, CHUNKS // 4)
        copy = pltpu.make_async_copy(err_ref.at[chunks], err_hbm.at[chunks], out_e.at[k])
        copy.start()
        outs.append(copy)
    for g in range(4):
        for q in range(4 * g, 4 * (g + 1)):
            lanes = slice(COLS * q, COLS * (q + 1))
            scaled = scaled_ref[q]
            first = BETA_ONE * first_ref[:, lanes] + (1.0 - BETA_ONE) * scaled
            second = BETA_TWO * second_ref[:, lanes] + (1.0 - BETA_TWO) * scaled * scaled
            first_res[:, lanes] = first
            second_res[:, lanes] = second
            direction_res[:, lanes] = first / (jnp.sqrt(second) + EPSILON)
        lanes = pl.ds(4 * COLS * g, 4 * COLS)
        for n, (res, hbm) in enumerate(
            ((first_res, first_hbm), (second_res, second_hbm), (direction_res, direction_hbm))
        ):
            copy = pltpu.make_async_copy(res.at[:, lanes], hbm.at[:, lanes], out_m.at[n, g])
            copy.start()
            outs.append(copy)
    for copy in outs:
        copy.wait()


def local(gradient, error_buffer, right_init, first_moment, second_moment):
    shape3 = (CHUNKS, ROWS, COLS)
    dma = pltpu.SemaphoreType.DMA
    vmem = pltpu.VMEM
    err, scaled = pl.pallas_call(
        kernel,
        out_shape=(jax.ShapeDtypeStruct(shape3, BF16), jax.ShapeDtypeStruct((SH, OWN, COLS), F32)),
        in_specs=[pl.BlockSpec(memory_space=pltpu.HBM)] * 3,
        out_specs=(pl.BlockSpec(memory_space=pltpu.VMEM),) * 2,
        scratch_shapes=[
            vmem((R, COLS), F32),
            vmem(shape3, BF16),
            vmem(shape3, BF16),
            vmem((2 * DP, 128, COLS), BF16),
            vmem((2 * DP, R, 128), F32),
            vmem((DP, R, 128), F32),
            vmem((DP, R, 128), F32),
            vmem((DP, R, 128), F32),
            vmem((ZN, R, 128), F32),
            vmem((2 * DP, R, 128), F32),
            vmem((2 * DP, 3 * R, 128), BF16),
            vmem((DP * SH, OWN, 128), BF16),
            vmem((DP, 8, 128), F32),
            vmem((DP, 8, 128), F32),
            vmem((DP, 8, 128), F32),
            vmem((2, DP, ZN, 8, 128), F32),
            vmem((2, ZN, 8, 128), F32),
            dma((CHUNKS,)), dma((CHUNKS,)), dma(()),
            dma((4,)), dma((4,)),
            dma((DP,)), dma((DP,)),
            dma((ZN,)), dma((ZN,)),
            dma((DP,)), dma((DP,)),
            dma((DP,)), dma((DP,)),
            dma((DP,)), dma((DP,)),
            dma((DP,)), dma((DP,)),
            dma((ZN,)), dma((ZN,)),
            dma((DP,)), dma((DP,)),
            dma((DP,)), dma((DP,)),
            dma((ZN,)), dma((ZN,)),
            dma((ZN,)), dma((ZN,)),
        ],
        compiler_params=pltpu.CompilerParams(
            collective_id=0, has_side_effects=True, vmem_limit_bytes=28 * 1024 * 1024
        ),
    )(
        *(
            pltpu.with_memory_space_constraint(t, pltpu.HBM)
            for t in (right_init.T, gradient.reshape(shape3), error_buffer.reshape(shape3))
        )
    )
    own = jax.ShapeDtypeStruct((OWN, F), F32)
    err, first, second, direction = pl.pallas_call(
        step_kernel,
        out_shape=(jax.ShapeDtypeStruct(shape3, BF16), own, own, own),
        in_specs=[pl.BlockSpec(memory_space=pl.ANY)] + [pl.BlockSpec(memory_space=pltpu.VMEM)] * 3,
        out_specs=(pl.BlockSpec(memory_space=pltpu.HBM),) * 4,
        scratch_shapes=[
            vmem((OWN, F), F32), vmem((OWN, F), F32), vmem((OWN, F), F32),
            dma((4,)), dma((3, 4)),
        ],
        compiler_params=pltpu.CompilerParams(vmem_limit_bytes=4 * 1024 * 1024),
    )(err, scaled, first_moment, second_moment)
    return (err.reshape(1, D, COLS), first, second, direction)


def solution(mesh):
    return jax.shard_map(
        local,
        mesh=mesh,
        in_specs=(
            P("dp", None, "shard"),
            P("dp", None, "shard"),
            P("shard", None),
            P(("dp", "shard"), None),
            P(("dp", "shard"), None),
        ),
        out_specs=(
            P("dp", None, "shard"),
            P(("dp", "shard"), None),
            P(("dp", "shard"), None),
            P(("dp", "shard"), None),
        ),
        check_vma=False,
    )
```

```python
import jax
import jax.numpy as jnp
from jax import lax
from jax.experimental import pallas as pl
from jax.experimental.pallas import tpu as pltpu
from jax.sharding import PartitionSpec as P

D = 4096
F = 6144
R = 32
DP = 16
SH = 16
ZN = 8
CHUNKS = 8
ROWS = D // CHUNKS
COLS = F // SH
OWN = D // (DP * SH)
PIECES = (R // 8) * (COLS // 128)
AHEAD = 3
PANEL = 8
EARLY = 3
HALF = 4

CLIP_LEVEL = 0.9
BETA_ONE = 0.9
BETA_TWO = 0.95
EPSILON = 1e-08

MESH = pl.DeviceIdType.MESH
F32 = jnp.float32
BF16 = jnp.bfloat16
NT = (((1,), (1,)), ((), ()))
NN = (((1,), (0,)), ((), ()))


def mm(a, b, dims):
    return lax.dot_general(a, b, dims, preferred_element_type=F32)


def split(x):
    high = x.astype(BF16)
    rest = x - high.astype(F32)
    mid = rest.astype(BF16)
    low = (rest - mid.astype(F32)).astype(BF16)
    return high, mid, low


def fold(full, n):
    rows = sum(full[R * a : R * (a + 1)] for a in range(n))
    return sum(rows[:, R * a : R * (a + 1)] for a in range(n))


def fold_lanes(wide):
    return wide[:, :R] + wide[:, R : 2 * R] + wide[:, 2 * R :]


def shifted_pair(gram_matrix):
    row = lax.broadcasted_iota(jnp.int32, (R, R), 0)
    col = lax.broadcasted_iota(jnp.int32, (R, R), 1)
    eye = row == col
    trace = jnp.sum(jnp.where(eye, gram_matrix, 0.0), keepdims=True)
    shifted = gram_matrix + jnp.where(eye, 1e-06 * trace / R, 0.0)
    return jnp.concatenate([shifted, jnp.where(eye, 1.0, 0.0)], axis=1)


def eliminate(work, panels):
    wide_row = lax.broadcasted_iota(jnp.int32, (R, 2 * R), 0)
    for k in panels:
        columns = [jnp.broadcast_to(work[:, k + b : k + b + 1], (R, 2 * R)) for b in range(PANEL)]
        rows = [work[k + b : k + b + 1] for b in range(PANEL)]
        for b in range(PANEL):
            inverse = 1.0 / columns[b][k + b : k + b + 1]
            line = rows[b] * inverse
            below = jnp.where(wide_row > k + b, columns[b], 0.0)
            for a in range(b + 1, PANEL):
                entry = columns[b][k + a : k + a + 1]
                columns[a] = columns[a] - columns[b] * (entry * inverse)
                rows[a] = rows[a] - entry * line
            work = work - below * line
    return work


def triangular_inverse(work):
    wide_row = lax.broadcasted_iota(jnp.int32, (R, 2 * R), 0)
    wide_col = lax.broadcasted_iota(jnp.int32, (R, 2 * R), 1)
    diagonal = jnp.sum(jnp.where(wide_row == wide_col, work, 0.0), axis=1, keepdims=True)
    return work[:, R : 2 * R] * lax.rsqrt(diagonal)


def kernel(
    right_hbm, grad_hbm, errb_hbm,
    err_ref, rows_ref, scale_ref,
    right_buf, grad_buf, errb_buf, merged, part, core_in, half, dp_in, z_in, left_raw,
    left_split, left_stack, right_out, right_in, right_all, planes, norms,
    load_g, load_e, load_m,
    s_core, r_core, s_dp, r_dp, s_z, r_z, s_dpa, r_dpa, s_ca, r_ca,
    s_rr, r_rr, s_ra, r_ra, s_bz, r_bz, s_pl, r_pl, s_bc, r_bc, s_nz, r_nz, s_nc, r_nc,
):
    i = lax.axis_index("dp")
    j = lax.axis_index("shard")
    x, y = i // 4, i % 4
    z, c = j // 2, j % 2
    other = j + 1 - 2 * c

    def dp_peer(d):
        return ((x + d // 4) % 4) * 4 + (y + d % 4) % 4

    def z_peer(d):
        return (z + d) % ZN

    def hops(d):
        return min(d // 4, 4 - d // 4) + min(d % 4, 4 - d % 4)

    dp_near = sorted(range(1, DP), key=hops)
    dp_far = dp_near[::-1]
    z_near = sorted(range(1, ZN), key=lambda d: min(d, ZN - d))
    z_far = z_near[::-1]

    def remote(src, dst, ss, rs, dp, sh):
        return pltpu.make_async_remote_copy(
            src_ref=src, dst_ref=dst, send_sem=ss, recv_sem=rs, device_id=(dp, sh), device_id_type=MESH
        )

    sends = []
    loads = []

    def send(*args):
        copy = remote(*args)
        copy.start()
        sends.append(copy)

    def finish():
        for copy in sends:
            copy.wait_send()
        sends.clear()

    barrier = pltpu.get_barrier_semaphore()
    for d in dp_far:
        pl.semaphore_signal(barrier, inc=1, device_id=(dp_peer(d), j), device_id_type=MESH)
    for d in z_far:
        pl.semaphore_signal(barrier, inc=1, device_id=(i, 2 * z_peer(d) + c), device_id_type=MESH)
    pl.semaphore_signal(barrier, inc=1, device_id=(i, other), device_id_type=MESH)
    load_right = pltpu.make_async_copy(right_hbm, right_buf, load_m)
    load_right.start()

    def load(k):
        a = pltpu.make_async_copy(grad_hbm.at[k], grad_buf.at[k], load_g.at[k])
        b = pltpu.make_async_copy(errb_hbm.at[k], errb_buf.at[k], load_e.at[k])
        a.start()
        b.start()
        loads.append((a, b))

    for k in range(AHEAD):
        load(k)

    load_right.wait()
    right_low = right_buf[...].astype(BF16)
    for k in range(CHUNKS):
        for copy in loads[k]:
            copy.wait()
        if k + AHEAD < CHUNKS:
            load(k + AHEAD)
        total = (grad_buf[k].astype(F32) + errb_buf[k].astype(F32)).astype(BF16)
        merged[4 * k : 4 * (k + 1)] = total.reshape(4, 128, COLS)
        product = mm(right_low, total, NT)
        for t in range(4):
            part[4 * k + t] = product[:, 128 * t : 128 * (t + 1)]

    pl.semaphore_wait(barrier, DP - 1 + ZN - 1 + 1)
    for k in range(4):
        send(part.at[pl.ds(DP * (1 - c) + 4 * k, 4)], core_in.at[pl.ds(4 * k, 4)], s_core.at[k], r_core.at[k], i, other)
    for k in range(4):
        remote(
            part.at[pl.ds(DP * c + 4 * k, 4)], core_in.at[pl.ds(4 * k, 4)], s_core.at[k], r_core.at[k], i, other
        ).wait_recv()
        for t in range(4 * k, 4 * k + 4):
            half[t] = part[DP * c + t] + core_in[t]
    for d in dp_far:
        p = dp_peer(d)
        send(half.at[p], dp_in.at[i], s_dp.at[d], r_dp.at[i], p, j)
    dp_in[i] = half[i]
    for d in dp_near:
        p = dp_peer(d)
        remote(half.at[p], dp_in.at[p], s_dp.at[d], r_dp.at[p], p, j).wait_recv()
    total = dp_in[0]
    for p in range(1, DP):
        total = total + dp_in[p]
    z_in[z] = total
    for d in z_far:
        p = z_peer(d)
        send(z_in.at[z], z_in.at[z], s_z.at[d], r_z.at[z], i, 2 * p + c)
    for d in z_near:
        p = z_peer(d)
        remote(z_in.at[p], z_in.at[p], s_z.at[d], r_z.at[p], i, 2 * p + c).wait_recv()
    total = z_in[0]
    for p in range(1, ZN):
        total = total + z_in[p]
    mine = DP * c + i
    left_raw[mine] = total * (1.0 / DP)
    for d in dp_far:
        send(left_raw.at[mine], left_raw.at[mine], s_dpa.at[d], r_dpa.at[i], dp_peer(d), j)
    send(left_raw.at[mine], left_raw.at[mine], s_ca.at[i], r_ca.at[i], i, other)

    def accumulate(sums, tiles):
        wide = jnp.concatenate([left_raw[q] for q in tiles], axis=1)
        stack = jnp.concatenate(split(wide), axis=0)
        for n, q in enumerate(tiles):
            left_split[q] = stack[:, 128 * n : 128 * (n + 1)]
        rows = jnp.concatenate([merged[q] for q in tiles], axis=0)
        return sums[0] + mm(stack, stack, NT), sums[1] + mm(stack, rows, NN)

    sums = jnp.zeros((3 * R, 3 * R), F32), jnp.zeros((3 * R, COLS), F32)
    order = [0] + dp_near
    for g in range(4):
        group = order[4 * g : 4 * (g + 1)]
        for d in group:
            p = dp_peer(d)
            q = DP * c + p
            if d:
                remote(left_raw.at[q], left_raw.at[q], s_dpa.at[d], r_dpa.at[p], p, j).wait_recv()
                send(left_raw.at[q], left_raw.at[q], s_ca.at[p], r_ca.at[p], i, other)
        sums = accumulate(sums, [DP * c + dp_peer(d) for d in group])
    for g in range(4):
        group = order[4 * g : 4 * (g + 1)]
        for d in group:
            p = dp_peer(d)
            q = DP * (1 - c) + p
            remote(left_raw.at[q], left_raw.at[q], s_ca.at[p], r_ca.at[p], i, other).wait_recv()
        sums = accumulate(sums, [DP * (1 - c) + dp_peer(d) for d in group])
    gram_sum, right_sum = sums
    right_part = right_sum[:R] + right_sum[R : 2 * R] + right_sum[2 * R :]
    for p in range(DP):
        g, t = (p % PIECES) // 3, p % 3
        right_out[p] = right_part[8 * g : 8 * (g + 1), 128 * t : 128 * (t + 1)]
    for d in dp_far:
        p = dp_peer(d)
        send(right_out.at[p], right_in.at[i], s_rr.at[d], r_rr.at[i], p, j)
    right_in[i] = right_out[i]
    panels = list(range(0, R, PANEL))
    work = eliminate(shifted_pair(fold(gram_sum, 3)), panels[:EARLY])
    for d in dp_near:
        p = dp_peer(d)
        remote(right_out.at[p], right_in.at[p], s_rr.at[d], r_rr.at[p], p, j).wait_recv()
    total = right_in[0]
    for p in range(1, DP):
        total = total + right_in[p]
    total = total * (1.0 / DP)
    right_all[i] = total
    planes[c, i, z] = total
    for d in z_far:
        send(planes.at[c, i, z], planes.at[c, i, z], s_bz.at[d], r_bz.at[z], i, 2 * z_peer(d) + c)
    for d in dp_far:
        send(right_all.at[i], right_all.at[i], s_ra.at[d], r_ra.at[i], dp_peer(d), j)
    inverse_parts = split(triangular_inverse(eliminate(work, panels[EARLY:])))
    inverse = jnp.concatenate([jnp.concatenate([t] * 3, axis=1) for t in inverse_parts], axis=0)

    def orthonormal(stack):
        wide = mm(inverse, stack, NN)
        return wide[:R] + wide[R : 2 * R] + wide[2 * R :]

    def left_rows(chunks, ortho_sum):
        for k in chunks:
            wide = jnp.concatenate([left_split[4 * k + t] for t in range(4)], axis=1)
            high, mid, _ = split(orthonormal(wide))
            stack = jnp.concatenate([high, mid], axis=0)
            ortho_sum = ortho_sum + mm(stack, stack, NT)
            left_stack[32 * k : 32 * (k + 1)] = jnp.concatenate([high, high, mid, mid], axis=0).T.reshape(32, OWN, 128)
        return ortho_sum

    ortho_sum = left_rows(range(HALF), jnp.zeros((2 * R, 2 * R), F32))
    for d in z_near:
        p = z_peer(d)
        remote(planes.at[c, i, p], planes.at[c, i, p], s_bz.at[d], r_bz.at[p], i, 2 * p + c).wait_recv()
    def spread():
        for d in dp_far:
            yield remote(planes.at[c, i], planes.at[c, i], s_pl.at[d], r_pl.at[i], dp_peer(d), j)
        yield remote(planes.at[c, i], planes.at[c, i], s_bc.at[i], r_bc.at[i], i, other)

    @pl.when(i < PIECES)
    def _():
        for copy in spread():
            copy.start()

    ortho_sum = left_rows(range(HALF, CHUNKS), ortho_sum)
    ortho_gram = fold(ortho_sum, 2)
    pick = (
        lax.broadcasted_iota(jnp.int32, (OWN, 128), 1)
        == lax.broadcasted_iota(jnp.int32, (OWN, 128), 0) + OWN * (j % 8)
    )
    own = mm(jnp.where(pick, 1.0, 0.0).astype(BF16), left_split[2 * i + j // 8], NT).astype(BF16)
    own = fold_lanes(mm(own, inverse, NT))
    own = mm(
        jnp.concatenate(split(own), axis=1),
        jnp.concatenate([jnp.concatenate([t] * 3, axis=0) for t in inverse_parts], axis=1),
        NN,
    )
    own = fold_lanes(own)
    finish()
    for d in dp_near:
        p = dp_peer(d)
        remote(right_all.at[p], right_all.at[p], s_ra.at[d], r_ra.at[p], p, j).wait_recv()

    def raw_stack(pieces):
        raw = jnp.concatenate(
            [jnp.concatenate([pieces[3 * g + t] for t in range(3)], axis=1) for g in range(R // 8)], axis=0
        )
        return jnp.concatenate(split(raw), axis=0)

    high, mid, _ = split(orthonormal(raw_stack([right_all[p] for p in range(PIECES)])))
    mine_stack = jnp.concatenate([high, mid, high, mid], axis=0)
    square = fold(mm(mine_stack[: 2 * R], mine_stack[: 2 * R], NT), 2)
    norms[c, z] = jnp.broadcast_to(jnp.sum(square * ortho_gram, keepdims=True), (8, 128))
    for d in z_far:
        send(norms.at[c, z], norms.at[c, z], s_nz.at[d], r_nz.at[z], i, 2 * z_peer(d) + c)
    send(norms.at[c, z], norms.at[c, z], s_nc.at[z], r_nc.at[z], i, other)
    for k in range(CHUNKS):
        rows = left_stack[32 * k : 32 * (k + 1)].reshape(ROWS, 128)
        whole = merged[4 * k : 4 * (k + 1)].reshape(ROWS, COLS)
        err_ref[k] = (whole.astype(F32) - mm(rows, mine_stack, NN)).astype(BF16)

    def relay(d):
        p = dp_peer(d)
        return p, remote(planes.at[c, p], planes.at[c, p], s_bc.at[p], r_bc.at[p], i, other)

    for d in dp_near:
        p, copy = relay(d)

        @pl.when(p < PIECES)
        def _():
            remote(planes.at[c, p], planes.at[c, p], s_pl.at[d], r_pl.at[p], p, j).wait_recv()
            copy.start()

    finish()

    @pl.when(i < PIECES)
    def _():
        for copy in spread():
            copy.wait_send()

    for d in z_near:
        p = z_peer(d)
        remote(norms.at[c, p], norms.at[c, p], s_nz.at[d], r_nz.at[p], i, 2 * p + c).wait_recv()
        send(norms.at[c, p], norms.at[c, p], s_nc.at[p], r_nc.at[p], i, other)
    own_stack = jnp.concatenate([jnp.concatenate([t] * 3, axis=1) for t in split(own)], axis=0)
    for n in range(2):
        core = c if n == 0 else 1 - c
        if n == 1:
            for p in range(PIECES):
                remote(planes.at[core, p], planes.at[core, p], s_bc.at[p], r_bc.at[p], i, other).wait_recv()
        for k in range(ZN):
            wide = mm(own_stack, raw_stack([planes[core, p, k] for p in range(PIECES)]), NN)
            rows_ref[2 * k + core] = wide[:OWN] + wide[OWN : 2 * OWN] + wide[2 * OWN :]
    for p in range(ZN):
        remote(norms.at[1 - c, p], norms.at[1 - c, p], s_nc.at[p], r_nc.at[p], i, other).wait_recv()
    total = norms[0, 0]
    for k in range(1, SH):
        total = total + norms[k // ZN, k % ZN]
    clip_level = CLIP_LEVEL * (float(R * (D + F)) ** 0.5)
    scale_ref[...] = clip_level / jnp.maximum(jnp.sqrt(total), clip_level)
    finish()
    for d in dp_near:
        p, copy = relay(d)

        @pl.when(p < PIECES)
        def _():
            copy.wait_send()


def step_kernel(
    err_ref, rows_ref, scale_ref, first_ref, second_ref, err_hbm, first_hbm, second_hbm, direction_hbm,
    first_res, second_res, direction_res, out_e, out_m,
):
    outs = []
    for k in range(4):
        chunks = pl.ds(k * CHUNKS // 4, CHUNKS // 4)
        copy = pltpu.make_async_copy(err_ref.at[chunks], err_hbm.at[chunks], out_e.at[k])
        copy.start()
        outs.append(copy)
    scale = scale_ref[0:1, 0:1]
    for g in range(4):
        for q in range(4 * g, 4 * (g + 1)):
            lanes = slice(COLS * q, COLS * (q + 1))
            scaled = rows_ref[q] * scale
            first = BETA_ONE * first_ref[:, lanes] + (1.0 - BETA_ONE) * scaled
            second = BETA_TWO * second_ref[:, lanes] + (1.0 - BETA_TWO) * scaled * scaled
            first_res[:, lanes] = first
            second_res[:, lanes] = second
            direction_res[:, lanes] = first / (jnp.sqrt(second) + EPSILON)
        lanes = pl.ds(4 * COLS * g, 4 * COLS)
        for n, (res, hbm) in enumerate(
            ((first_res, first_hbm), (second_res, second_hbm), (direction_res, direction_hbm))
        ):
            copy = pltpu.make_async_copy(res.at[:, lanes], hbm.at[:, lanes], out_m.at[n, g])
            copy.start()
            outs.append(copy)
    for copy in outs:
        copy.wait()


def local(gradient, error_buffer, right_init, first_moment, second_moment):
    shape3 = (CHUNKS, ROWS, COLS)
    dma = pltpu.SemaphoreType.DMA
    vmem = pltpu.VMEM
    err, rows, scale = pl.pallas_call(
        kernel,
        out_shape=(jax.ShapeDtypeStruct(shape3, BF16), jax.ShapeDtypeStruct((SH, OWN, COLS), F32), jax.ShapeDtypeStruct((8, 128), F32)),
        in_specs=[pl.BlockSpec(memory_space=pltpu.HBM)] * 3,
        out_specs=(pl.BlockSpec(memory_space=pltpu.VMEM),) * 3,
        scratch_shapes=[
            vmem((R, COLS), F32),
            vmem(shape3, BF16),
            vmem(shape3, BF16),
            vmem((2 * DP, 128, COLS), BF16),
            vmem((2 * DP, R, 128), F32),
            vmem((DP, R, 128), F32),
            vmem((DP, R, 128), F32),
            vmem((DP, R, 128), F32),
            vmem((ZN, R, 128), F32),
            vmem((2 * DP, R, 128), F32),
            vmem((2 * DP, 3 * R, 128), BF16),
            vmem((DP * SH, OWN, 128), BF16),
            vmem((DP, 8, 128), F32),
            vmem((DP, 8, 128), F32),
            vmem((DP, 8, 128), F32),
            vmem((2, DP, ZN, 8, 128), F32),
            vmem((2, ZN, 8, 128), F32),
            dma((CHUNKS,)), dma((CHUNKS,)), dma(()),
            dma((4,)), dma((4,)),
            dma((DP,)), dma((DP,)),
            dma((ZN,)), dma((ZN,)),
            dma((DP,)), dma((DP,)),
            dma((DP,)), dma((DP,)),
            dma((DP,)), dma((DP,)),
            dma((DP,)), dma((DP,)),
            dma((ZN,)), dma((ZN,)),
            dma((DP,)), dma((DP,)),
            dma((DP,)), dma((DP,)),
            dma((ZN,)), dma((ZN,)),
            dma((ZN,)), dma((ZN,)),
        ],
        compiler_params=pltpu.CompilerParams(
            collective_id=0, has_side_effects=True, vmem_limit_bytes=28 * 1024 * 1024
        ),
    )(
        *(
            pltpu.with_memory_space_constraint(t, pltpu.HBM)
            for t in (right_init.T, gradient.reshape(shape3), error_buffer.reshape(shape3))
        )
    )
    own = jax.ShapeDtypeStruct((OWN, F), F32)
    err, first, second, direction = pl.pallas_call(
        step_kernel,
        out_shape=(jax.ShapeDtypeStruct(shape3, BF16), own, own, own),
        in_specs=[pl.BlockSpec(memory_space=pl.ANY)] + [pl.BlockSpec(memory_space=pltpu.VMEM)] * 4,
        out_specs=(pl.BlockSpec(memory_space=pltpu.HBM),) * 4,
        scratch_shapes=[
            vmem((OWN, F), F32), vmem((OWN, F), F32), vmem((OWN, F), F32),
            dma((4,)), dma((3, 4)),
        ],
        compiler_params=pltpu.CompilerParams(vmem_limit_bytes=4 * 1024 * 1024),
    )(err, rows, scale, first_moment, second_moment)
    return (err.reshape(1, D, COLS), first, second, direction)


def solution(mesh):
    return jax.shard_map(
        local,
        mesh=mesh,
        in_specs=(
            P("dp", None, "shard"),
            P("dp", None, "shard"),
            P("shard", None),
            P(("dp", "shard"), None),
            P(("dp", "shard"), None),
        ),
        out_specs=(
            P("dp", None, "shard"),
            P(("dp", "shard"), None),
            P(("dp", "shard"), None),
            P(("dp", "shard"), None),
        ),
        check_vma=False,
    )
```

```python
import jax
import jax.numpy as jnp
from jax import lax
from jax.experimental import pallas as pl
from jax.experimental.pallas import tpu as pltpu
from jax.sharding import PartitionSpec as P

D = 4096
F = 6144
R = 32
DP = 16
SH = 16
ZN = 8
CHUNKS = 8
ROWS = D // CHUNKS
COLS = F // SH
OWN = D // (DP * SH)
PIECES = (R // 8) * (COLS // 128)
AHEAD = 3
PANEL = 8
EARLY = 3
HALF = 4

CLIP_LEVEL = 0.9
BETA_ONE = 0.9
BETA_TWO = 0.95
EPSILON = 1e-08

MESH = pl.DeviceIdType.MESH
F32 = jnp.float32
BF16 = jnp.bfloat16
NT = (((1,), (1,)), ((), ()))
NN = (((1,), (0,)), ((), ()))


def mm(a, b, dims):
    return lax.dot_general(a, b, dims, preferred_element_type=F32)


def split(x):
    high = x.astype(BF16)
    rest = x - high.astype(F32)
    mid = rest.astype(BF16)
    low = (rest - mid.astype(F32)).astype(BF16)
    return high, mid, low


def fold(full, n):
    rows = sum(full[R * a : R * (a + 1)] for a in range(n))
    return sum(rows[:, R * a : R * (a + 1)] for a in range(n))


def fold_lanes(wide):
    return wide[:, :R] + wide[:, R : 2 * R] + wide[:, 2 * R :]


def shifted_pair(gram_matrix):
    row = lax.broadcasted_iota(jnp.int32, (R, R), 0)
    col = lax.broadcasted_iota(jnp.int32, (R, R), 1)
    eye = row == col
    trace = jnp.sum(jnp.where(eye, gram_matrix, 0.0), keepdims=True)
    shifted = gram_matrix + jnp.where(eye, 1e-06 * trace / R, 0.0)
    return jnp.concatenate([shifted, jnp.where(eye, 1.0, 0.0)], axis=1)


def eliminate(work, panels):
    wide_row = lax.broadcasted_iota(jnp.int32, (R, 2 * R), 0)
    for k in panels:
        columns = [jnp.broadcast_to(work[:, k + b : k + b + 1], (R, 2 * R)) for b in range(PANEL)]
        rows = [work[k + b : k + b + 1] for b in range(PANEL)]
        for b in range(PANEL):
            inverse = 1.0 / columns[b][k + b : k + b + 1]
            line = rows[b] * inverse
            below = jnp.where(wide_row > k + b, columns[b], 0.0)
            for a in range(b + 1, PANEL):
                entry = columns[b][k + a : k + a + 1]
                columns[a] = columns[a] - columns[b] * (entry * inverse)
                rows[a] = rows[a] - entry * line
            work = work - below * line
    return work


def triangular_inverse(work):
    wide_row = lax.broadcasted_iota(jnp.int32, (R, 2 * R), 0)
    wide_col = lax.broadcasted_iota(jnp.int32, (R, 2 * R), 1)
    diagonal = jnp.sum(jnp.where(wide_row == wide_col, work, 0.0), axis=1, keepdims=True)
    return work[:, R : 2 * R] * lax.rsqrt(diagonal)


def kernel(
    right_hbm, grad_hbm, errb_hbm,
    err_ref, rows_ref, scale_ref,
    right_buf, grad_buf, errb_buf, merged, part, core_in, half, dp_in, z_in, left_raw,
    left_split, left_stack, right_out, right_in, right_all, planes, norms,
    load_g, load_e, load_m,
    s_core, r_core, s_dp, r_dp, s_z, r_z, s_dpa, r_dpa, s_ca, r_ca,
    s_rr, r_rr, s_ra, r_ra, s_bz, r_bz, s_pl, r_pl, s_bc, r_bc, s_nz, r_nz, s_nc, r_nc,
):
    i = lax.axis_index("dp")
    j = lax.axis_index("shard")
    x, y = i // 4, i % 4
    z, c = j // 2, j % 2
    other = j + 1 - 2 * c

    def dp_peer(d):
        return ((x + d // 4) % 4) * 4 + (y + d % 4) % 4

    def z_peer(d):
        return (z + d) % ZN

    def hops(d):
        return min(d // 4, 4 - d // 4) + min(d % 4, 4 - d % 4)

    dp_near = sorted(range(1, DP), key=hops)
    dp_far = dp_near[::-1]
    z_near = sorted(range(1, ZN), key=lambda d: min(d, ZN - d))
    z_far = z_near[::-1]

    def remote(src, dst, ss, rs, dp, sh):
        return pltpu.make_async_remote_copy(
            src_ref=src, dst_ref=dst, send_sem=ss, recv_sem=rs, device_id=(dp, sh), device_id_type=MESH
        )

    sends = []
    loads = []

    def send(*args):
        copy = remote(*args)
        copy.start()
        sends.append(copy)

    def finish():
        for copy in sends:
            copy.wait_send()
        sends.clear()

    barrier = pltpu.get_barrier_semaphore()
    for d in dp_far:
        pl.semaphore_signal(barrier, inc=1, device_id=(dp_peer(d), j), device_id_type=MESH)
    for d in z_far:
        pl.semaphore_signal(barrier, inc=1, device_id=(i, 2 * z_peer(d) + c), device_id_type=MESH)
    pl.semaphore_signal(barrier, inc=1, device_id=(i, other), device_id_type=MESH)
    load_right = pltpu.make_async_copy(right_hbm, right_buf, load_m)
    load_right.start()

    def load(k):
        a = pltpu.make_async_copy(grad_hbm.at[k], grad_buf.at[k], load_g.at[k])
        b = pltpu.make_async_copy(errb_hbm.at[k], errb_buf.at[k], load_e.at[k])
        a.start()
        b.start()
        loads.append((a, b))

    for k in range(AHEAD):
        load(k)

    load_right.wait()
    right_low = right_buf[...].astype(BF16)
    for k in range(CHUNKS):
        for copy in loads[k]:
            copy.wait()
        if k + AHEAD < CHUNKS:
            load(k + AHEAD)
        total = (grad_buf[k].astype(F32) + errb_buf[k].astype(F32)).astype(BF16)
        merged[4 * k : 4 * (k + 1)] = total.reshape(4, 128, COLS)
        product = mm(right_low, total, NT)
        for t in range(4):
            part[4 * k + t] = product[:, 128 * t : 128 * (t + 1)]

    pl.semaphore_wait(barrier, DP - 1 + ZN - 1 + 1)
    x_order = (2, 1, 3, 0)

    def piece(k):
        return 4 * ((x + x_order[k]) % 4)

    for k in range(4):
        q = piece(k)
        send(part.at[pl.ds(DP * (1 - c) + q, 4)], core_in.at[pl.ds(q, 4)], s_core.at[k], r_core.at[k], i, other)
    for k in range(4):
        q = piece(k)
        remote(
            part.at[pl.ds(DP * c + q, 4)], core_in.at[pl.ds(q, 4)], s_core.at[k], r_core.at[k], i, other
        ).wait_recv()
        for t in range(4):
            half[q + t] = part[DP * c + q + t] + core_in[q + t]
        for dy in (2, 1, 3, 0):
            d = 4 * x_order[k] + dy
            if d:
                p = dp_peer(d)
                send(half.at[p], dp_in.at[i], s_dp.at[d], r_dp.at[i], p, j)
    dp_in[i] = half[i]
    for d in dp_near:
        p = dp_peer(d)
        remote(half.at[p], dp_in.at[p], s_dp.at[d], r_dp.at[p], p, j).wait_recv()
    total = dp_in[0]
    for p in range(1, DP):
        total = total + dp_in[p]
    z_in[z] = total
    for d in z_far:
        p = z_peer(d)
        send(z_in.at[z], z_in.at[z], s_z.at[d], r_z.at[z], i, 2 * p + c)
    for d in z_near:
        p = z_peer(d)
        remote(z_in.at[p], z_in.at[p], s_z.at[d], r_z.at[p], i, 2 * p + c).wait_recv()
    total = z_in[0]
    for p in range(1, ZN):
        total = total + z_in[p]
    mine = DP * c + i
    left_raw[mine] = total * (1.0 / DP)
    for d in dp_far:
        send(left_raw.at[mine], left_raw.at[mine], s_dpa.at[d], r_dpa.at[i], dp_peer(d), j)
    send(left_raw.at[mine], left_raw.at[mine], s_ca.at[i], r_ca.at[i], i, other)

    def accumulate(sums, tiles):
        wide = jnp.concatenate([left_raw[q] for q in tiles], axis=1)
        stack = jnp.concatenate(split(wide), axis=0)
        for n, q in enumerate(tiles):
            left_split[q] = stack[:, 128 * n : 128 * (n + 1)]
        rows = jnp.concatenate([merged[q] for q in tiles], axis=0)
        return sums[0] + mm(stack, stack, NT), sums[1] + mm(stack, rows, NN)

    sums = jnp.zeros((3 * R, 3 * R), F32), jnp.zeros((3 * R, COLS), F32)
    order = [0] + dp_near
    for g in range(4):
        group = order[4 * g : 4 * (g + 1)]
        for d in group:
            p = dp_peer(d)
            q = DP * c + p
            if d:
                remote(left_raw.at[q], left_raw.at[q], s_dpa.at[d], r_dpa.at[p], p, j).wait_recv()
                send(left_raw.at[q], left_raw.at[q], s_ca.at[p], r_ca.at[p], i, other)
        sums = accumulate(sums, [DP * c + dp_peer(d) for d in group])
    for g in range(4):
        group = order[4 * g : 4 * (g + 1)]
        for d in group:
            p = dp_peer(d)
            q = DP * (1 - c) + p
            remote(left_raw.at[q], left_raw.at[q], s_ca.at[p], r_ca.at[p], i, other).wait_recv()
        sums = accumulate(sums, [DP * (1 - c) + dp_peer(d) for d in group])
    gram_sum, right_sum = sums
    right_part = right_sum[:R] + right_sum[R : 2 * R] + right_sum[2 * R :]
    for p in range(DP):
        g, t = (p % PIECES) // 3, p % 3
        right_out[p] = right_part[8 * g : 8 * (g + 1), 128 * t : 128 * (t + 1)]
    for d in dp_far:
        p = dp_peer(d)
        send(right_out.at[p], right_in.at[i], s_rr.at[d], r_rr.at[i], p, j)
    right_in[i] = right_out[i]
    panels = list(range(0, R, PANEL))
    work = eliminate(shifted_pair(fold(gram_sum, 3)), panels[:EARLY])
    for d in dp_near:
        p = dp_peer(d)
        remote(right_out.at[p], right_in.at[p], s_rr.at[d], r_rr.at[p], p, j).wait_recv()
    total = right_in[0]
    for p in range(1, DP):
        total = total + right_in[p]
    total = total * (1.0 / DP)
    right_all[i] = total
    planes[c, i, z] = total
    for d in z_far:
        send(planes.at[c, i, z], planes.at[c, i, z], s_bz.at[d], r_bz.at[z], i, 2 * z_peer(d) + c)
    for d in dp_far:
        send(right_all.at[i], right_all.at[i], s_ra.at[d], r_ra.at[i], dp_peer(d), j)
    inverse_parts = split(triangular_inverse(eliminate(work, panels[EARLY:])))
    inverse = jnp.concatenate([jnp.concatenate([t] * 3, axis=1) for t in inverse_parts], axis=0)

    def orthonormal(stack):
        wide = mm(inverse, stack, NN)
        return wide[:R] + wide[R : 2 * R] + wide[2 * R :]

    def left_rows(chunks, ortho_sum):
        for k in chunks:
            wide = jnp.concatenate([left_split[4 * k + t] for t in range(4)], axis=1)
            high, mid, _ = split(orthonormal(wide))
            stack = jnp.concatenate([high, mid], axis=0)
            ortho_sum = ortho_sum + mm(stack, stack, NT)
            left_stack[32 * k : 32 * (k + 1)] = jnp.concatenate([high, high, mid, mid], axis=0).T.reshape(32, OWN, 128)
        return ortho_sum

    ortho_sum = left_rows(range(HALF), jnp.zeros((2 * R, 2 * R), F32))
    for d in z_near:
        p = z_peer(d)
        remote(planes.at[c, i, p], planes.at[c, i, p], s_bz.at[d], r_bz.at[p], i, 2 * p + c).wait_recv()
    def spread():
        for d in dp_far:
            yield remote(planes.at[c, i], planes.at[c, i], s_pl.at[d], r_pl.at[i], dp_peer(d), j)
        yield remote(planes.at[c, i], planes.at[c, i], s_bc.at[i], r_bc.at[i], i, other)

    @pl.when(i < PIECES)
    def _():
        for copy in spread():
            copy.start()

    ortho_sum = left_rows(range(HALF, CHUNKS), ortho_sum)
    ortho_gram = fold(ortho_sum, 2)
    pick = (
        lax.broadcasted_iota(jnp.int32, (OWN, 128), 1)
        == lax.broadcasted_iota(jnp.int32, (OWN, 128), 0) + OWN * (j % 8)
    )
    own = mm(jnp.where(pick, 1.0, 0.0).astype(BF16), left_split[2 * i + j // 8], NT).astype(BF16)
    own = fold_lanes(mm(own, inverse, NT))
    own = mm(
        jnp.concatenate(split(own), axis=1),
        jnp.concatenate([jnp.concatenate([t] * 3, axis=0) for t in inverse_parts], axis=1),
        NN,
    )
    own = fold_lanes(own)
    finish()
    for d in dp_near:
        p = dp_peer(d)
        remote(right_all.at[p], right_all.at[p], s_ra.at[d], r_ra.at[p], p, j).wait_recv()

    def raw_stack(pieces):
        raw = jnp.concatenate(
            [jnp.concatenate([pieces[3 * g + t] for t in range(3)], axis=1) for g in range(R // 8)], axis=0
        )
        return jnp.concatenate(split(raw), axis=0)

    high, mid, _ = split(orthonormal(raw_stack([right_all[p] for p in range(PIECES)])))
    mine_stack = jnp.concatenate([high, mid, high, mid], axis=0)
    square = fold(mm(mine_stack[: 2 * R], mine_stack[: 2 * R], NT), 2)
    norms[c, z] = jnp.broadcast_to(jnp.sum(square * ortho_gram, keepdims=True), (8, 128))
    for d in z_far:
        send(norms.at[c, z], norms.at[c, z], s_nz.at[d], r_nz.at[z], i, 2 * z_peer(d) + c)
    send(norms.at[c, z], norms.at[c, z], s_nc.at[z], r_nc.at[z], i, other)
    for k in range(CHUNKS):
        rows = left_stack[32 * k : 32 * (k + 1)].reshape(ROWS, 128)
        whole = merged[4 * k : 4 * (k + 1)].reshape(ROWS, COLS)
        err_ref[k] = (whole.astype(F32) - mm(rows, mine_stack, NN)).astype(BF16)

    def relay(d):
        p = dp_peer(d)
        return p, remote(planes.at[c, p], planes.at[c, p], s_bc.at[p], r_bc.at[p], i, other)

    for d in dp_near:
        p, copy = relay(d)

        @pl.when(p < PIECES)
        def _():
            remote(planes.at[c, p], planes.at[c, p], s_pl.at[d], r_pl.at[p], p, j).wait_recv()
            copy.start()

    finish()

    @pl.when(i < PIECES)
    def _():
        for copy in spread():
            copy.wait_send()

    for d in z_near:
        p = z_peer(d)
        remote(norms.at[c, p], norms.at[c, p], s_nz.at[d], r_nz.at[p], i, 2 * p + c).wait_recv()
        send(norms.at[c, p], norms.at[c, p], s_nc.at[p], r_nc.at[p], i, other)
    own_stack = jnp.concatenate([jnp.concatenate([t] * 3, axis=1) for t in split(own)], axis=0)
    for n in range(2):
        core = c if n == 0 else 1 - c
        if n == 1:
            for p in range(PIECES):
                remote(planes.at[core, p], planes.at[core, p], s_bc.at[p], r_bc.at[p], i, other).wait_recv()
        for k in range(ZN):
            wide = mm(own_stack, raw_stack([planes[core, p, k] for p in range(PIECES)]), NN)
            rows_ref[2 * k + core] = wide[:OWN] + wide[OWN : 2 * OWN] + wide[2 * OWN :]
    for p in range(ZN):
        remote(norms.at[1 - c, p], norms.at[1 - c, p], s_nc.at[p], r_nc.at[p], i, other).wait_recv()
    total = norms[0, 0]
    for k in range(1, SH):
        total = total + norms[k // ZN, k % ZN]
    clip_level = CLIP_LEVEL * (float(R * (D + F)) ** 0.5)
    scale_ref[...] = clip_level / jnp.maximum(jnp.sqrt(total), clip_level)
    finish()
    for d in dp_near:
        p, copy = relay(d)

        @pl.when(p < PIECES)
        def _():
            copy.wait_send()


def step_kernel(
    err_ref, rows_ref, scale_ref, first_ref, second_ref, err_hbm, first_hbm, second_hbm, direction_hbm,
    first_res, second_res, direction_res, out_e, out_m,
):
    outs = []
    for k in range(4):
        chunks = pl.ds(k * CHUNKS // 4, CHUNKS // 4)
        copy = pltpu.make_async_copy(err_ref.at[chunks], err_hbm.at[chunks], out_e.at[k])
        copy.start()
        outs.append(copy)
    scale = scale_ref[0:1, 0:1]
    for g in range(4):
        for q in range(4 * g, 4 * (g + 1)):
            lanes = slice(COLS * q, COLS * (q + 1))
            scaled = rows_ref[q] * scale
            first = BETA_ONE * first_ref[:, lanes] + (1.0 - BETA_ONE) * scaled
            second = BETA_TWO * second_ref[:, lanes] + (1.0 - BETA_TWO) * scaled * scaled
            first_res[:, lanes] = first
            second_res[:, lanes] = second
            direction_res[:, lanes] = first / (jnp.sqrt(second) + EPSILON)
        lanes = pl.ds(4 * COLS * g, 4 * COLS)
        for n, (res, hbm) in enumerate(
            ((first_res, first_hbm), (second_res, second_hbm), (direction_res, direction_hbm))
        ):
            copy = pltpu.make_async_copy(res.at[:, lanes], hbm.at[:, lanes], out_m.at[n, g])
            copy.start()
            outs.append(copy)
    for copy in outs:
        copy.wait()


def local(gradient, error_buffer, right_init, first_moment, second_moment):
    shape3 = (CHUNKS, ROWS, COLS)
    dma = pltpu.SemaphoreType.DMA
    vmem = pltpu.VMEM
    err, rows, scale = pl.pallas_call(
        kernel,
        out_shape=(jax.ShapeDtypeStruct(shape3, BF16), jax.ShapeDtypeStruct((SH, OWN, COLS), F32), jax.ShapeDtypeStruct((8, 128), F32)),
        in_specs=[pl.BlockSpec(memory_space=pltpu.HBM)] * 3,
        out_specs=(pl.BlockSpec(memory_space=pltpu.VMEM),) * 3,
        scratch_shapes=[
            vmem((R, COLS), F32),
            vmem(shape3, BF16),
            vmem(shape3, BF16),
            vmem((2 * DP, 128, COLS), BF16),
            vmem((2 * DP, R, 128), F32),
            vmem((DP, R, 128), F32),
            vmem((DP, R, 128), F32),
            vmem((DP, R, 128), F32),
            vmem((ZN, R, 128), F32),
            vmem((2 * DP, R, 128), F32),
            vmem((2 * DP, 3 * R, 128), BF16),
            vmem((DP * SH, OWN, 128), BF16),
            vmem((DP, 8, 128), F32),
            vmem((DP, 8, 128), F32),
            vmem((DP, 8, 128), F32),
            vmem((2, DP, ZN, 8, 128), F32),
            vmem((2, ZN, 8, 128), F32),
            dma((CHUNKS,)), dma((CHUNKS,)), dma(()),
            dma((4,)), dma((4,)),
            dma((DP,)), dma((DP,)),
            dma((ZN,)), dma((ZN,)),
            dma((DP,)), dma((DP,)),
            dma((DP,)), dma((DP,)),
            dma((DP,)), dma((DP,)),
            dma((DP,)), dma((DP,)),
            dma((ZN,)), dma((ZN,)),
            dma((DP,)), dma((DP,)),
            dma((DP,)), dma((DP,)),
            dma((ZN,)), dma((ZN,)),
            dma((ZN,)), dma((ZN,)),
        ],
        compiler_params=pltpu.CompilerParams(
            collective_id=0, has_side_effects=True, vmem_limit_bytes=28 * 1024 * 1024
        ),
    )(
        *(
            pltpu.with_memory_space_constraint(t, pltpu.HBM)
            for t in (right_init.T, gradient.reshape(shape3), error_buffer.reshape(shape3))
        )
    )
    own = jax.ShapeDtypeStruct((OWN, F), F32)
    err, first, second, direction = pl.pallas_call(
        step_kernel,
        out_shape=(jax.ShapeDtypeStruct(shape3, BF16), own, own, own),
        in_specs=[pl.BlockSpec(memory_space=pl.ANY)] + [pl.BlockSpec(memory_space=pltpu.VMEM)] * 4,
        out_specs=(pl.BlockSpec(memory_space=pltpu.HBM),) * 4,
        scratch_shapes=[
            vmem((OWN, F), F32), vmem((OWN, F), F32), vmem((OWN, F), F32),
            dma((4,)), dma((3, 4)),
        ],
        compiler_params=pltpu.CompilerParams(vmem_limit_bytes=4 * 1024 * 1024),
    )(err, rows, scale, first_moment, second_moment)
    return (err.reshape(1, D, COLS), first, second, direction)


def solution(mesh):
    return jax.shard_map(
        local,
        mesh=mesh,
        in_specs=(
            P("dp", None, "shard"),
            P("dp", None, "shard"),
            P("shard", None),
            P(("dp", "shard"), None),
            P(("dp", "shard"), None),
        ),
        out_specs=(
            P("dp", None, "shard"),
            P(("dp", "shard"), None),
            P(("dp", "shard"), None),
            P(("dp", "shard"), None),
        ),
        check_vma=False,
    )
```
